256 devices in a mesh: space: 64 (over z, y, core), rhs: 4 (over x).
Axes of the slice: x: 4, y: 4, z: 8, core: 2. Of those that a mesh axis runs over, the one named last changes fastest.
Arguments:
- rhs_vec: float32 [64, 65536], P('rhs', 'space'), may hold values from -40 to 40
- self_coef: float32 [65536], P('space'), may hold values from 2 to 4
- near_mats: bfloat16 [512, 8, 128, 128], P('space'), may hold values from -0.1875 to 0.1875
- near_ids: int32 [512, 8], P('space'), may hold values from 0 to 511, as said below
- near_count: int32 [512], P('space'), may hold values from 3 to 8, as said below
- interp: bfloat16 [512, 128, 32], P('space'), may hold values from -0.5 to 0.5
- skel_idx: int32 [512, 32], P('space'), may hold values from 0 to 127, as said below
- coupling: bfloat16 [16384, 4, 4096], P('space', 'rhs'), may hold values from -0.0234375 to 0.0234375
- diag_prec: float32 [65536], P('space'), may hold values from 1.5 to 4
- low_rank: float32 [65536, 512], P('space'), may hold values from -0.010481569 to 0.010481569
Outputs:
- solution: float32 [64, 65536], P('rhs', 'space')
The draws below stay inside these ranges and needn't reach their ends.
Inputs may be any that keep to these rules, and one draw needn't show every extreme that they name: `near_ids`: slot 0 of each block names the block itself, slot 1 a block of the region before it (of its own region for the first region), slot 2 a block of the region after it (of its own region for the last region); every entry names a block of the same 8-block region or of the region before or after it. `near_count`: some regions use all 8 slots in every block. `skel_idx`: each row holds 32 distinct panel numbers of its block, rising.
All inputs are finite; a program needn't handle non-finite values.
Results may differ from the reference program's by a relative error of at most 0.001.
Values may be sent and summed in bfloat16 or wider, within the bound.
A program may use at most 64 MiB of HBM per device.

```python
import math
import jax
import jax.numpy as jnp
from jax import lax

BLK = 128
RANK = 32
LOWR = 512
EXC = 64
K_MAX = 8
NB_DEV = 8
NBLOCKS = 512
PANELS = 65536
SKQ = 64
NSKEL = 16384
N_SPACE = 64
N_RHS = 4


def factor_draw(key):
    scale_one = (PANELS * 5 // 4) ** (-0.5)
    base = jnp.clip(jax.random.normal(jax.random.fold_in(key, 41), (PANELS, LOWR), jnp.float32), -3.0, 3.0)
    return base * scale_one


def draw_low_rank(key, part):
    return factor_draw(key)


def draw_rhs_vec(key, part):
    factor = factor_draw(key)
    mix_scale = math.sqrt(10.0 * PANELS / LOWR)
    mixing = jax.random.normal(jax.random.fold_in(key, 42), (LOWR, EXC), jnp.float32) * mix_scale
    aligned = jnp.transpose(jnp.dot(factor, mixing, precision=lax.Precision.HIGHEST))
    noise = jnp.clip(jax.random.normal(jax.random.fold_in(key, 43), (EXC, PANELS), jnp.float32), -6.0, 6.0) * 4.0
    return jnp.clip(noise + aligned, -40.0, 40.0)


def draw_near_ids(key, part):
    block = jnp.arange(NBLOCKS, dtype=jnp.int32)
    region = block // NB_DEV
    last_region = NBLOCKS // NB_DEV - 1
    lowest = jnp.maximum(0, (region - 1) * NB_DEV)
    highest = jnp.minimum(NBLOCKS, (region + 2) * NB_DEV)
    raw_ids = jax.random.randint(jax.random.fold_in(key, 21), (NBLOCKS, K_MAX), 0, 3 * NB_DEV)
    chosen = lowest[:, None] + raw_ids % (highest - lowest)[:, None]
    side_raw = jax.random.randint(jax.random.fold_in(key, 22), (NBLOCKS, 2), 0, NB_DEV)
    before = jnp.maximum(region - 1, 0) * NB_DEV + side_raw[:, 0]
    after = jnp.minimum(region + 1, last_region) * NB_DEV + side_raw[:, 1]
    chosen = chosen.at[:, 0].set(block)
    chosen = chosen.at[:, 1].set(before)
    chosen = chosen.at[:, 2].set(after)
    return chosen.astype(jnp.int32)


def draw_near_count(key, part):
    heavy = jax.random.randint(jax.random.fold_in(key, 11), (NBLOCKS // NB_DEV,), 0, 4) == 0
    heavy = heavy.at[0].set(True)
    light = jax.random.randint(jax.random.fold_in(key, 12), (NBLOCKS,), 3, max(4, K_MAX // 2 + 1))
    heavy_blocks = jnp.repeat(heavy, NB_DEV)
    return jnp.where(heavy_blocks, K_MAX, light).astype(jnp.int32)


def draw_skel_idx(key, part):
    row_keys = jax.random.split(jax.random.fold_in(key, 31), NBLOCKS)
    chosen = jax.vmap(lambda row_key: jax.random.permutation(row_key, BLK)[:RANK])(row_keys)
    return jnp.sort(chosen, axis=1).astype(jnp.int32)


def block_scale(stream_key, dims, cuts, low, largest):
    level, own = 1.0, jax.random.fold_in(stream_key, 6)
    for dim, blocks in cuts:
        heights = jnp.exp(jax.random.uniform(jax.random.fold_in(own, dim), (blocks,), jnp.float32, low / len(cuts), largest / len(cuts)))
        level = level * jnp.repeat(heights, dims[dim] // blocks).reshape([-1 if axis == dim else 1 for axis in range(len(dims))])
    return level


def gaussian(key, dims, deviation, limit, cuts=(), kind=jnp.bfloat16):
    array = deviation * jax.random.normal(key, dims, jnp.float32)
    if cuts:
        array = array * block_scale(key, dims, cuts, -0.22, 0.18)
    return jnp.clip(array, -limit, limit).astype(kind)


def setup_inputs(seed: int = 0) -> dict:
    key_list = jax.random.split(jax.random.key(seed), 11)
    rhs_vec = draw_rhs_vec(jax.random.fold_in(key_list[10], 71), 0)
    self_coef = jnp.clip(jnp.exp(math.log(4.0) - 0.6931472 * jax.random.uniform(key_list[1], (PANELS,), jnp.float32) ** block_scale(key_list[1], (PANELS,), ((0, 64),), -0.2, 0.2)), 2.0, 4.0)
    near_mats = gaussian(key_list[2], (NBLOCKS, K_MAX, BLK, BLK), (BLK * K_MAX) ** -0.5, 0.1875, ((0, 64),))
    near_ids = draw_near_ids(jax.random.fold_in(key_list[10], 71), 0)
    near_count = draw_near_count(jax.random.fold_in(key_list[10], 71), 0)
    interp = gaussian(key_list[5], (NBLOCKS, BLK, RANK), BLK ** -0.5, 0.5, ((0, 64),))
    skel_idx = draw_skel_idx(jax.random.fold_in(key_list[10], 71), 0)
    coupling = gaussian(key_list[7], (NSKEL, N_RHS, N_SPACE * SKQ), (4 * NSKEL) ** -0.5, 0.0234375, ((0, 64), (1, 4)))
    diag_prec = jnp.clip(jnp.exp(math.log(4.0) - 0.98082925 * jax.random.uniform(key_list[8], (PANELS,), jnp.float32) ** block_scale(key_list[8], (PANELS,), ((0, 64),), -0.2, 0.2)), 1.5, 4.0)
    low_rank = draw_low_rank(jax.random.fold_in(key_list[10], 71), 0)
    return {"rhs_vec": rhs_vec, "self_coef": self_coef, "near_mats": near_mats, "near_ids": near_ids, "near_count": near_count, "interp": interp, "skel_idx": skel_idx, "coupling": coupling, "diag_prec": diag_prec, "low_rank": low_rank}


HIGH = lax.Precision.HIGHEST
EPS = 1e-06

def givens_pair(start_len, diag_one, below_one, upper_two, diag_two, below_two):
    radius_one = jnp.sqrt(diag_one * diag_one + below_one * below_one)
    cos_one = diag_one / radius_one
    sin_one = below_one / radius_one
    upper = cos_one * upper_two + sin_one * diag_two
    lower = cos_one * diag_two - sin_one * upper_two
    radius_two = jnp.sqrt(lower * lower + below_two * below_two)
    step_two = lower / radius_two * (-sin_one * start_len) / radius_two
    step_one = (cos_one * start_len - upper * step_two) / radius_one
    return (step_one, step_two)

def reference(rhs_vec, self_coef, near_mats, near_ids, near_count, interp, skel_idx, coupling, diag_prec, low_rank):
    excitations = rhs_vec.shape[0]
    onehot = (skel_idx[:, :, None] == jnp.arange(BLK, dtype=jnp.int32)[None, None, :]).astype(jnp.float32)
    restrict = onehot + jnp.swapaxes(interp.astype(jnp.float32), 1, 2)
    live_slots = (jnp.arange(K_MAX, dtype=jnp.int32)[None, :] < near_count[:, None]).astype(jnp.bfloat16)
    slot_mats = near_mats.astype(jnp.float32)
    coupling_blocks = coupling.reshape(NBLOCKS, RANK, N_RHS, N_SPACE * SKQ)

    def precond(vector):
        projected = jnp.dot(vector, low_rank, precision=HIGH)
        return diag_prec[None, :] * vector - jnp.dot(projected, low_rank.T, precision=HIGH)

    def operate(field):
        field_low = field.astype(jnp.bfloat16)
        blocks = field_low.reshape(excitations, NBLOCKS, BLK)

        def near_row(row_blocks):
            picked = row_blocks[near_ids] * live_slots[:, :, None]
            return jnp.einsum('bkij,bkj->bi', slot_mats, picked.astype(jnp.float32), precision=HIGH)
        near = lax.map(near_row, blocks)
        charges = jnp.einsum('brj,ebj->ebr', restrict, blocks.astype(jnp.float32), precision=HIGH)
        packed = charges.astype(jnp.bfloat16).reshape(excitations, N_SPACE, N_RHS, SKQ)
        charges_in = jnp.transpose(packed, (0, 2, 1, 3)).reshape(excitations, N_RHS, N_SPACE * SKQ).astype(jnp.float32)

        def far_block(rows):
            return jnp.einsum('gqc,eqc->eg', rows.astype(jnp.float32), charges_in, precision=HIGH)
        far_field = jnp.transpose(lax.map(far_block, coupling_blocks), (1, 0, 2))
        far_pot = jnp.einsum('brj,ebr->ebj', restrict, far_field, precision=HIGH)
        return self_coef[None, :] * field + near.reshape(excitations, PANELS) + far_pot.reshape(excitations, PANELS)
    start_len = jnp.sqrt(lax.optimization_barrier(jnp.sum(rhs_vec * rhs_vec, axis=1)) + EPS)
    first_dir = rhs_vec / start_len[:, None]
    first_pre = precond(first_dir)
    residue = operate(first_pre)
    diag_one = lax.optimization_barrier(jnp.sum(residue * first_dir, axis=1))
    residue = residue - diag_one[:, None] * first_dir
    below_one = jnp.sqrt(lax.optimization_barrier(jnp.sum(residue * residue, axis=1)) + EPS)
    second_dir = residue / below_one[:, None]
    second_pre = precond(second_dir)
    residue = operate(second_pre)
    upper_two = lax.optimization_barrier(jnp.sum(residue * first_dir, axis=1))
    diag_two = lax.optimization_barrier(jnp.sum(residue * second_dir, axis=1))
    residue = residue - upper_two[:, None] * first_dir
    residue = residue - diag_two[:, None] * second_dir
    below_two = jnp.sqrt(lax.optimization_barrier(jnp.sum(residue * residue, axis=1)) + EPS)
    step_one, step_two = givens_pair(start_len, diag_one, below_one, upper_two, diag_two, below_two)
    return step_one[:, None] * first_pre + step_two[:, None] * second_pre
```

```python
import jax
import jax.numpy as jnp
from jax import lax
from jax.experimental import pallas as pl
from jax.experimental.pallas import tpu as pltpu
from jax.sharding import PartitionSpec as P

EPS = 1e-06
F32 = jnp.float32
BF16 = jnp.bfloat16
MESH = pl.DeviceIdType.MESH

(SIB, YAX, ZAX, BACK, STAT, NEAR, CHARGE, GATHER, FAR) = range(9)
PHASES = 9
COUPLE = 2 * PHASES
FINAL = COUPLE + 1
(L_RHS, L_U, L_DIAG, L_SELF, L_INTERP, L_SKEL, L_NEAR, L_COUPLE) = range(8)


def dot_nn(a, b):
    return lax.dot_general(a, b, (((1,), (0,)), ((), ())), preferred_element_type=F32)


def dot_nt(a, b):
    return lax.dot_general(a, b, (((1,), (1,)), ((), ())), preferred_element_type=F32)


def halves(value):
    high = value.astype(BF16)
    return high, (value - high.astype(F32)).astype(BF16)


def lane_sum(value):
    return jnp.sum(value, axis=1, keepdims=True)


def kernel(
    rhs_hbm, self_hbm, near_hbm, ids_ref, count_ref, interp_hbm, skel_hbm, couple_hbm,
    diag_hbm, u_hbm, out_ref,
    rhs_ref, self_ref, near_ref, interp_ref, skel_ref, couple_ref, diag_ref, u_ref,
    u_high, u_low, pick_ref, put_ref, z_ref, w_ref,
    part_ref, sib_ref, y_ref, zax_ref, full_ref, row_ref, stat_ref,
    ext_ref, charge_out, charge_in, gather_ref, far_out, far_in,
    send_sems, recv_sems, local_sems,
):
    s = lax.axis_index("space")
    x = lax.axis_index("rhs")
    z = s // 8
    y = (s // 2) % 4
    c = s % 2
    oc = 1 - c
    chip = s // 2
    sibling = (chip * 2 + oc, x)

    def local(src, dst, index):
        return pltpu.make_async_copy(src, dst, local_sems.at[index])

    loads = [
        local(rhs_hbm, rhs_ref, L_RHS),
        local(u_hbm, u_ref, L_U),
        local(diag_hbm, diag_ref, L_DIAG),
        local(self_hbm, self_ref, L_SELF),
        local(interp_hbm, interp_ref, L_INTERP),
        local(skel_hbm, skel_ref, L_SKEL),
        local(near_hbm, near_ref, L_NEAR),
        local(couple_hbm, couple_ref.at[c], L_COUPLE),
    ]
    for load in loads:
        load.start()

    barrier = pltpu.get_barrier_semaphore()

    def greet(step, carry):
        pl.semaphore_signal(
            barrier, inc=1, device_id=((s + step) % 64, x), device_id_type=MESH
        )
        return carry

    lax.fori_loop(1, 64, greet, 0)
    for dx in (1, 2, 3):
        for dc in (0, 1):
            pl.semaphore_signal(
                barrier,
                inc=1,
                device_id=(chip * 2 + (c + dc) % 2, (x + dx) % 4),
                device_id_type=MESH,
            )

    def remote(src, dst, phase, device):
        return pltpu.make_async_remote_copy(
            src_ref=src,
            dst_ref=dst,
            send_sem=send_sems.at[phase],
            recv_sem=recv_sems.at[phase],
            device_id=device,
            device_id_type=MESH,
        )

    def arrived(ref, phase):
        remote(ref, ref, phase, sibling).wait_recv()

    def sent(ref, phase):
        remote(ref, ref, phase, sibling).wait_send()

    lane = lax.broadcasted_iota(jnp.int32, (16, 128), 1)
    excitation = lax.broadcasted_iota(jnp.int32, (16, 128), 0)

    def row_of(fields):
        total = jnp.zeros((16, 128), F32)
        for index, field in enumerate(fields):
            total = total + jnp.where(lane == index * 16 + excitation, field, 0.0)
        return jnp.sum(total, axis=0, keepdims=True)

    def column_of(row):
        return lane_sum(jnp.where(lane == excitation, row, 0.0))

    def project(value):
        high, low = halves(value)
        both = dot_nn(jnp.concatenate([high, low], axis=0), u_high[...])
        return both[:16] + both[16:] + dot_nn(high, u_low[...])

    def expand(coeffs):
        high, low = halves(coeffs)
        both = dot_nt(jnp.concatenate([high, low], axis=0), u_high[...])
        return both[:16] + both[16:] + dot_nt(high, u_low[...])

    def send_stats(index, phase, fields):
        row_ref[index] = row_of(fields)
        stat_ref[index, pl.ds(s, 1), :] = row_ref[index]

        def tell(step, carry):
            remote(
                row_ref.at[index],
                stat_ref.at[index, pl.ds(s, 1), :],
                phase,
                ((s + step) % 64, x),
            ).start()
            return carry

        lax.fori_loop(1, 64, tell, 0)

    def read_stats(index, phase):
        arrived(stat_ref.at[index, pl.ds(0, 63), :], phase)
        return stat_ref[index]

    def all_reduce(m, partial, between):
        base = m * PHASES
        part_ref[m, 0] = partial[:, :256]
        part_ref[m, 1] = partial[:, 256:]
        remote(part_ref.at[m, oc], sib_ref.at[m], base + SIB, sibling).start()
        arrived(sib_ref.at[m], base + SIB)
        y_ref[m, 0] = part_ref[m, c] + sib_ref[m]
        for dy in (1, 2, 3):
            remote(
                y_ref.at[m, 0],
                y_ref.at[m, dy],
                base + YAX,
                ((z * 4 + (y + dy) % 4) * 2 + c, x),
            ).start()
        between()
        arrived(y_ref.at[m, pl.ds(1, 3)], base + YAX)
        zax_ref[m, 0] = (y_ref[m, 0] + y_ref[m, 1]) + (y_ref[m, 2] + y_ref[m, 3])
        for dz in range(1, 8):
            remote(
                zax_ref.at[m, 0],
                zax_ref.at[m, dz],
                base + ZAX,
                ((((z + dz) % 8) * 4 + y) * 2 + c, x),
            ).start()
        arrived(zax_ref.at[m, pl.ds(1, 7)], base + ZAX)
        pairs = [zax_ref[m, 2 * i] + zax_ref[m, 2 * i + 1] for i in range(4)]
        full_ref[m, c] = (pairs[0] + pairs[1]) + (pairs[2] + pairs[3])
        remote(full_ref.at[m, c], full_ref.at[m, c], base + BACK, sibling).start()
        arrived(full_ref.at[m, oc], base + BACK)
        return jnp.concatenate([full_ref[m, 0], full_ref[m, 1]], axis=1)

    def operate(m):
        base = m * PHASES
        field = z_ref[m]
        low = field.astype(BF16)
        for b in range(8):
            ext_ref[m, 8 + b] = low[:, 128 * b : 128 * (b + 1)]
        remote(
            ext_ref.at[m, pl.ds(8, 8)], ext_ref.at[m, pl.ds(0, 8)], base + NEAR, ((s + 1) % 64, x)
        ).start()
        remote(
            ext_ref.at[m, pl.ds(8, 8)], ext_ref.at[m, pl.ds(16, 8)], base + NEAR, ((s + 63) % 64, x)
        ).start()
        charges = []
        for half in range(2):
            part = low[:, 512 * half : 512 * (half + 1)]
            charges.append(dot_nt(part, pick_ref[half]) + dot_nt(part, put_ref[half]))
        for quarter in range(4):
            tile = charges[quarter // 2]
            tile = jnp.where(c == quarter % 2, tile, pltpu.roll(tile, 64, 1))
            tile = jnp.where(lane // 64 == c, tile, 0.0)
            charge_out[m, quarter, 0] = tile[:8]
            charge_out[m, quarter, 1] = tile[8:]
        mine = x * 2 + c
        others = [(dx, dc) for dx in range(4) for dc in range(2) if dx or dc]
        for dx, dc in others:
            to_x, to_c = (x + dx) % 4, (c + dc) % 2
            remote(
                charge_out.at[m, to_x, to_c],
                charge_in.at[m, mine],
                base + CHARGE,
                (chip * 2 + to_c, to_x),
            ).start()
        charge_in[m, mine] = charge_out[m, x, c]
        arrived(charge_in.at[m, pl.ds(0, 7)], base + CHARGE)
        block = jnp.concatenate(
            [charge_in[m, 2 * i] + charge_in[m, 2 * i + 1] for i in range(4)], axis=0
        ).astype(BF16)
        own = pl.ds(pl.multiple_of(chip * 128, 128), 128)
        gather_ref[m, :, own] = block

        def spread(step, carry):
            remote(
                gather_ref.at[m, :, own],
                gather_ref.at[m, :, own],
                base + GATHER,
                (((chip + step) % 32) * 2 + c, x),
            ).start()
            return carry

        lax.fori_loop(1, 32, spread, 0)

        if m == 0:
            loads[L_NEAR].wait()
        arrived(ext_ref.at[m, pl.ds(0, 16)], base + NEAR)
        for b in range(8):
            total = jnp.zeros((16, 128), F32)
            for pair in range(4):
                sides = []
                for k in (2 * pair, 2 * pair + 1):
                    source = jnp.clip(ids_ref[b, k] - (s - 1) * 8, 0, 23)
                    live = (k < count_ref[b]).astype(F32)
                    sides.append((ext_ref[m, source].astype(F32) * live).astype(BF16))
                mats = jnp.concatenate([near_ref[b, 2 * pair], near_ref[b, 2 * pair + 1]], axis=1)
                total = total + dot_nt(jnp.concatenate(sides, axis=1), mats)
            columns = slice(128 * b, 128 * (b + 1))
            w_ref[:, columns] = total + self_ref[:, columns] * field[:, columns]

        if m == 0:
            loads[L_COUPLE].wait()
            arrived(couple_ref.at[oc], COUPLE)
        arrived(gather_ref.at[m, :, pl.ds(0, 31 * 128)], base + GATHER)
        for side in range(2):
            part = dot_nt(gather_ref[m], couple_ref[side])
            for i in range(4):
                far_out[m, side, i] = part[8 * i : 8 * (i + 1)]
        for dx, dc in others:
            to_x, to_c = (x + dx) % 4, (c + dc) % 2
            remote(
                far_out.at[m, to_c, to_x],
                far_in.at[m, mine],
                base + FAR,
                (chip * 2 + to_c, to_x),
            ).start()
        far_in[m, mine] = far_out[m, c, x]
        arrived(far_in.at[m, pl.ds(0, 7)], base + FAR)
        far = jnp.concatenate(
            [
                (far_in[m, i] + far_in[m, 2 + i]) + (far_in[m, 4 + i] + far_in[m, 6 + i])
                for i in range(2)
            ],
            axis=0,
        )
        results = []
        for half in range(2):
            part = far[:, 128 * half : 128 * (half + 1)]
            high, rest = halves(part)
            rest_high, rest_low = halves(part - high.astype(F32))
            stack = jnp.concatenate([high, rest_high, rest_low], axis=0)
            spread_out = dot_nn(stack, pick_ref[half]) + dot_nn(stack, put_ref[half])
            results.append(spread_out[:16] + spread_out[16:32] + spread_out[32:])
        return w_ref[...] + jnp.concatenate(results, axis=1)

    loads[L_RHS].wait()
    loads[L_U].wait()
    factor = u_ref[...]
    factor_high, factor_low = halves(factor)
    u_high[...] = factor_high
    u_low[...] = factor_low
    rhs = rhs_ref[...]
    partial = project(rhs)
    for index in (L_DIAG, L_SELF, L_INTERP, L_SKEL):
        loads[index].wait()

    pl.semaphore_wait(barrier, 69)

    def start_rest():
        send_stats(0, STAT, [lane_sum(rhs * rhs)])
        remote(couple_hbm, couple_ref.at[c], COUPLE, sibling).start()
        pick_ref[...] = jnp.zeros(pick_ref.shape, BF16)
        put_ref[...] = jnp.zeros(put_ref.shape, BF16)
        square = lax.broadcasted_iota(jnp.int32, (32, 32), 0)
        square = (square == lax.broadcasted_iota(jnp.int32, (32, 32), 1)).astype(F32)
        turned = dot_nt(square.astype(BF16), skel_ref[...].astype(F32).astype(BF16))
        panel = lax.broadcasted_iota(jnp.int32, (32, 128), 1).astype(F32)
        for b in range(8):
            rows = slice(32 * (b % 4), 32 * (b % 4 + 1))
            columns = slice(128 * (b % 4), 128 * (b % 4 + 1))
            chosen = (panel == turned[:, b : b + 1]).astype(F32)
            pick_ref[b // 4, rows, columns] = chosen.astype(BF16)
            put_ref[b // 4, rows, columns] = interp_ref[b]

    raw = all_reduce(0, partial, start_rest)
    total = jnp.sum(read_stats(0, STAT), axis=0, keepdims=True)
    beta_row = jnp.sqrt(total + EPS)
    beta = column_of(beta_row)
    first = rhs / beta
    first_coeffs = raw / beta
    diag = diag_ref[...]
    z_ref[0] = diag * first - expand(first_coeffs)
    norm_one = lane_sum(first * first)
    safe_one = jnp.where(norm_one > 1e-12, norm_one, 1.0)

    def along(inner, norm, safe):
        return jnp.where(norm > 1e-12, inner / safe, 0.0)

    residue = operate(0)

    def first_stats():
        own = along(lane_sum(residue * first), norm_one, safe_one)
        rest = residue - own * first
        send_stats(
            1, PHASES + STAT, [own, lane_sum(rest * first), norm_one, lane_sum(rest * rest)]
        )

    raw = all_reduce(1, project(residue), first_stats)
    stats = read_stats(1, PHASES + STAT)

    def fields_of(stats, count):
        return [stats] + [pltpu.roll(stats, 128 - 16 * i, 1) for i in range(1, count)]

    def rows_sum(value):
        return jnp.sum(value, axis=0, keepdims=True)

    own, cross, norm, rest = fields_of(stats, 4)
    h11_row = rows_sum(cross + own * norm)
    shift = own - h11_row
    square = rows_sum(rest + 2.0 * shift * cross + shift * shift * norm)
    h21_row = jnp.sqrt(jnp.maximum(square, 0.0) + EPS)
    h11 = column_of(h11_row)
    h21 = column_of(h21_row)
    second = (residue - h11 * first) / h21
    second_coeffs = (raw - h11 * first_coeffs) / h21
    z_ref[1] = diag * second - expand(second_coeffs)
    norm_two = lane_sum(second * second)
    mixed = lane_sum(first * second)
    safe_two = jnp.where(norm_two > 1e-12, norm_two, 1.0)

    residue = operate(1)
    own_one = along(lane_sum(residue * first), norm_one, safe_one)
    rest = residue - own_one * first
    own_two = along(lane_sum(rest * second), norm_two, safe_two)
    rest = rest - own_two * second
    send_stats(
        2,
        FINAL,
        [
            own_one, own_two, lane_sum(rest * first), lane_sum(rest * second),
            norm_one, mixed, norm_two, lane_sum(rest * rest),
        ],
    )
    stats = read_stats(2, FINAL)
    own_one, own_two, cross_one, cross_two, n11, n12, n22, rest = fields_of(stats, 8)
    h12_row = rows_sum(cross_one + own_one * n11 + own_two * n12)
    h22_row = rows_sum(cross_two + own_one * n12 + own_two * n22)
    shift_one = own_one - h12_row
    shift_two = own_two - h22_row
    square = rows_sum(
        rest
        + 2.0 * (shift_one * cross_one + shift_two * cross_two)
        + shift_one * shift_one * n11
        + 2.0 * shift_one * shift_two * n12
        + shift_two * shift_two * n22
    )
    h32_row = jnp.sqrt(jnp.maximum(square, 0.0) + EPS)
    radius_one = jnp.sqrt(h11_row * h11_row + h21_row * h21_row)
    cos_one = h11_row / radius_one
    sin_one = h21_row / radius_one
    upper = cos_one * h12_row + sin_one * h22_row
    lower = cos_one * h22_row - sin_one * h12_row
    radius_two = jnp.sqrt(lower * lower + h32_row * h32_row)
    step_two = lower / radius_two * (-sin_one * beta_row) / radius_two
    step_one = (cos_one * beta_row - upper * step_two) / radius_one
    out_ref[...] = column_of(step_one) * z_ref[0] + column_of(step_two) * z_ref[1]

    sent(couple_ref.at[c], COUPLE)
    sent(stat_ref.at[2, pl.ds(0, 63), :], FINAL)
    for m in range(2):
        base = m * PHASES
        sent(sib_ref.at[m], base + SIB)
        sent(y_ref.at[m, pl.ds(1, 3)], base + YAX)
        sent(zax_ref.at[m, pl.ds(1, 7)], base + ZAX)
        sent(full_ref.at[m, c], base + BACK)
        sent(stat_ref.at[m, pl.ds(0, 63), :], base + STAT)
        sent(ext_ref.at[m, pl.ds(0, 16)], base + NEAR)
        sent(charge_in.at[m, pl.ds(0, 7)], base + CHARGE)
        sent(gather_ref.at[m, :, pl.ds(0, 31 * 128)], base + GATHER)
        sent(far_in.at[m, pl.ds(0, 7)], base + FAR)


def on_device(
    rhs_vec, self_coef, near_mats, near_ids, near_count, interp, skel_idx, coupling,
    diag_prec, low_rank,
):
    anywhere = pl.BlockSpec(memory_space=pl.ANY)
    scalars = pl.BlockSpec(memory_space=pltpu.SMEM)
    vmem = pltpu.VMEM
    return pl.pallas_call(
        kernel,
        out_shape=jax.ShapeDtypeStruct((16, 1024), F32),
        in_specs=[
            anywhere, anywhere, anywhere, scalars, scalars, anywhere, anywhere, anywhere,
            anywhere, anywhere,
        ],
        out_specs=pl.BlockSpec(memory_space=pltpu.VMEM),
        scratch_shapes=[
            vmem((16, 1024), F32),
            vmem((1, 1024), F32),
            vmem((8, 8, 128, 128), BF16),
            vmem((8, 32, 128), BF16),
            vmem((8, 32), jnp.int32),
            vmem((2, 256, 4096), BF16),
            vmem((1, 1024), F32),
            vmem((1024, 512), F32),
            vmem((1024, 512), BF16),
            vmem((1024, 512), BF16),
            vmem((2, 128, 512), BF16),
            vmem((2, 128, 512), BF16),
            vmem((2, 16, 1024), F32),
            vmem((16, 1024), F32),
            vmem((2, 2, 16, 256), F32),
            vmem((2, 16, 256), F32),
            vmem((2, 4, 16, 256), F32),
            vmem((2, 8, 16, 256), F32),
            vmem((2, 2, 16, 256), F32),
            vmem((3, 1, 128), F32),
            vmem((3, 64, 128), F32),
            vmem((2, 24, 16, 128), BF16),
            vmem((2, 4, 2, 8, 128), F32),
            vmem((2, 8, 8, 128), F32),
            vmem((2, 32, 4096), BF16),
            vmem((2, 2, 4, 8, 256), F32),
            vmem((2, 8, 8, 256), F32),
            pltpu.SemaphoreType.DMA((FINAL + 1,)),
            pltpu.SemaphoreType.DMA((FINAL + 1,)),
            pltpu.SemaphoreType.DMA((8,)),
        ],
        compiler_params=pltpu.CompilerParams(
            collective_id=0, has_side_effects=True, vmem_limit_bytes=56 * 1024 * 1024
        ),
        name="gmres",
    )(
        rhs_vec,
        self_coef.reshape(1, -1),
        near_mats,
        near_ids,
        near_count,
        jnp.swapaxes(interp, 1, 2),
        skel_idx,
        coupling.reshape(coupling.shape[0], coupling.shape[2]),
        diag_prec.reshape(1, -1),
        low_rank,
    )


def solution(mesh):
    placed = (
        P("rhs", "space"),
        P("space"),
        P("space", None, None, None),
        P("space", None),
        P("space"),
        P("space", None, None),
        P("space", None),
        P("space", "rhs", None),
        P("space"),
        P("space", None),
    )
    return jax.shard_map(
        on_device, mesh=mesh, in_specs=placed, out_specs=P("rhs", "space"), check_vma=False
    )
```

```python
import jax
import jax.numpy as jnp
from jax import lax
from jax.experimental import pallas as pl
from jax.experimental.pallas import tpu as pltpu
from jax.sharding import PartitionSpec as P

EPS = 1e-06
F32 = jnp.float32
BF16 = jnp.bfloat16
MESH = pl.DeviceIdType.MESH

(SIB, YAX, ZAX, BACK, STAT, NEAR, CHARGE, FAR, LINE) = range(9)
PLANE = LINE + 8
ROW_SIB = PLANE + 4
ROW_Y = ROW_SIB + 1
ROW_Z = ROW_SIB + 2
PHASES = ROW_SIB + 3
COUPLE = 2 * PHASES
FINAL = COUPLE + 1
FOUR = (2, 1, 3)
EIGHT = (4, 3, 5, 2, 6, 1, 7)
CROSS = ((2, 1), (2, 0), (1, 1), (3, 1), (1, 0), (3, 0), (0, 1))
(L_RHS, L_U, L_DIAG, L_SELF, L_INTERP, L_SKEL, L_NEAR, L_COUPLE) = range(8)


def dot_nn(a, b):
    return lax.dot_general(a, b, (((1,), (0,)), ((), ())), preferred_element_type=F32)


def dot_nt(a, b):
    return lax.dot_general(a, b, (((1,), (1,)), ((), ())), preferred_element_type=F32)


def halves(value):
    high = value.astype(BF16)
    return high, (value - high.astype(F32)).astype(BF16)


def lane_sum(value):
    return jnp.sum(value, axis=1, keepdims=True)


def kernel(
    rhs_hbm, self_hbm, near_hbm, ids_ref, count_ref, interp_hbm, skel_hbm, couple_hbm,
    diag_hbm, u_hbm, out_ref,
    rhs_ref, self_ref, near_ref, interp_ref, skel_ref, couple_ref, diag_ref, u_ref,
    u_high, u_low, pick_ref, put_ref, z_ref, w_ref,
    part_ref, sib_ref, y_ref, zax_ref, full_ref, line_ref, row_ref, stat_ref,
    ext_ref, charge_out, charge_in, gather_ref, far_out, far_in,
    send_sems, recv_sems, local_sems,
):
    s = lax.axis_index("space")
    x = lax.axis_index("rhs")
    z = s // 8
    y = (s // 2) % 4
    c = s % 2
    oc = 1 - c
    chip = s // 2
    sibling = (chip * 2 + oc, x)

    def local(src, dst, index):
        return pltpu.make_async_copy(src, dst, local_sems.at[index])

    loads = [
        local(rhs_hbm, rhs_ref, L_RHS),
        local(u_hbm, u_ref, L_U),
        local(diag_hbm, diag_ref, L_DIAG),
        local(self_hbm, self_ref, L_SELF),
        local(interp_hbm, interp_ref, L_INTERP),
        local(skel_hbm, skel_ref, L_SKEL),
        local(near_hbm, near_ref, L_NEAR),
    ]
    for load in loads:
        load.start()

    def load_columns(line, carry):
        for row in range(4):
            source = pl.multiple_of((line * 4 + row) * 128, 128)
            local(
                couple_hbm.at[:, pl.ds(source, 128)],
                couple_ref.at[c, row, :, pl.ds(pl.multiple_of(line * 128, 128), 128)],
                L_COUPLE,
            ).start()
        return carry

    lax.fori_loop(0, 8, load_columns, 0)

    barrier = pltpu.get_barrier_semaphore()

    def at(dz=0, dy=0, dc=0):
        return ((((z + dz) % 8) * 4 + (y + dy) % 4) * 2 + (c + dc) % 2, x)

    def across(dx, dc):
        return (chip * 2 + (c + dc) % 2, (x + dx) % 4)

    greeted = [at(dz=dz) for dz in EIGHT] + [at(dy=dy) for dy in FOUR]
    greeted += [across(dx, dc) for dx, dc in CROSS]
    for device in greeted:
        pl.semaphore_signal(barrier, inc=1, device_id=device, device_id_type=MESH)

    def remote(src, dst, phase, device):
        return pltpu.make_async_remote_copy(
            src_ref=src,
            dst_ref=dst,
            send_sem=send_sems.at[phase],
            recv_sem=recv_sems.at[phase],
            device_id=device,
            device_id_type=MESH,
        )

    def arrived(ref, phase):
        remote(ref, ref, phase, sibling).wait_recv()

    def sent(ref, phase):
        remote(ref, ref, phase, sibling).wait_send()

    lane = lax.broadcasted_iota(jnp.int32, (16, 128), 1)
    excitation = lax.broadcasted_iota(jnp.int32, (16, 128), 0)

    def row_of(fields):
        total = jnp.zeros((16, 128), F32)
        for index, field in enumerate(fields):
            total = total + jnp.where(lane == index * 16 + excitation, field, 0.0)
        return jnp.sum(total, axis=0, keepdims=True)

    def column_of(row):
        return lane_sum(jnp.where(lane == excitation, row, 0.0))

    def project(value):
        high, low = halves(value)
        both = dot_nn(jnp.concatenate([high, low], axis=0), u_high[...])
        return both[:16] + both[16:] + dot_nn(high, u_low[...])

    def expand(coeffs):
        high, low = halves(coeffs)
        both = dot_nt(jnp.concatenate([high, low], axis=0), u_high[...])
        return both[:16] + both[16:] + dot_nt(high, u_low[...])

    def send_stats(index, phase, fields):
        row_ref[index] = row_of(fields)
        stat_ref[index, pl.ds(s, 1), :] = row_ref[index]

        def tell(step, carry):
            dz = (4 + (step % 2 * -2 + 1) * ((step + 1) // 2)) % 8
            for dy in (2, 1, 3):
                for dc in (1, 0):
                    remote(
                        row_ref.at[index], stat_ref.at[index, pl.ds(s, 1), :], phase,
                        at(dz, dy, dc),
                    ).start()
            remote(
                row_ref.at[index], stat_ref.at[index, pl.ds(s, 1), :], phase, at(dz, 0, 1)
            ).start()
            return carry

        lax.fori_loop(0, 8, tell, 0)
        for dz in EIGHT:
            remote(
                row_ref.at[index], stat_ref.at[index, pl.ds(s, 1), :], phase, at(dz)
            ).start()

    def read_stats(index, phase):
        arrived(stat_ref.at[index, pl.ds(0, 63), :], phase)
        return stat_ref[index]

    def all_reduce(m, partial, between, row=None):
        base = m * PHASES
        part_ref[m, 0] = partial[:, :256]
        part_ref[m, 1] = partial[:, 256:]
        remote(part_ref.at[m, oc], sib_ref.at[m], base + SIB, at(dc=1)).start()
        if row is not None:
            line_ref[0] = row
            remote(line_ref.at[0], line_ref.at[1], base + ROW_SIB, at(dc=1)).start()
        arrived(sib_ref.at[m], base + SIB)
        y_ref[m, 0] = part_ref[m, c] + sib_ref[m]
        for dy in FOUR:
            remote(y_ref.at[m, 0], y_ref.at[m, dy], base + YAX, at(dy=dy)).start()
        if row is not None:
            arrived(line_ref.at[1], base + ROW_SIB)
            line_ref[2] = line_ref[0] + line_ref[1]
            for dy in FOUR:
                remote(line_ref.at[2], line_ref.at[2 + dy], base + ROW_Y, at(dy=dy)).start()
        between()
        arrived(y_ref.at[m, pl.ds(1, 3)], base + YAX)
        zax_ref[m, 0] = (y_ref[m, 0] + y_ref[m, 1]) + (y_ref[m, 2] + y_ref[m, 3])
        for dz in EIGHT:
            remote(zax_ref.at[m, 0], zax_ref.at[m, dz], base + ZAX, at(dz=dz)).start()
        if row is not None:
            arrived(line_ref.at[pl.ds(3, 3)], base + ROW_Y)
            line_ref[6] = (line_ref[2] + line_ref[3]) + (line_ref[4] + line_ref[5])
            for dz in EIGHT:
                remote(line_ref.at[6], line_ref.at[6 + dz], base + ROW_Z, at(dz=dz)).start()
        arrived(zax_ref.at[m, pl.ds(1, 7)], base + ZAX)
        pairs = [zax_ref[m, 2 * i] + zax_ref[m, 2 * i + 1] for i in range(4)]
        full_ref[m, c] = (pairs[0] + pairs[1]) + (pairs[2] + pairs[3])
        remote(full_ref.at[m, c], full_ref.at[m, c], base + BACK, at(dc=1)).start()
        if row is not None:
            arrived(line_ref.at[pl.ds(7, 7)], base + ROW_Z)
            pairs = [line_ref[6 + 2 * i] + line_ref[7 + 2 * i] for i in range(4)]
            row = (pairs[0] + pairs[1]) + (pairs[2] + pairs[3])
        arrived(full_ref.at[m, oc], base + BACK)
        return jnp.concatenate([full_ref[m, 0], full_ref[m, 1]], axis=1), row

    def operate(m):
        base = m * PHASES
        field = z_ref[m]
        low = field.astype(BF16)
        for b in range(8):
            ext_ref[m, 8 + b] = low[:, 128 * b : 128 * (b + 1)]
        remote(
            ext_ref.at[m, pl.ds(8, 8)], ext_ref.at[m, pl.ds(0, 8)], base + NEAR, ((s + 1) % 64, x)
        ).start()
        remote(
            ext_ref.at[m, pl.ds(8, 8)], ext_ref.at[m, pl.ds(16, 8)], base + NEAR, ((s + 63) % 64, x)
        ).start()
        charges = []
        for half in range(2):
            part = low[:, 512 * half : 512 * (half + 1)]
            charges.append(dot_nt(part, pick_ref[half]) + dot_nt(part, put_ref[half]))
        for quarter in range(4):
            tile = charges[quarter // 2]
            tile = jnp.where(c == quarter % 2, tile, pltpu.roll(tile, 64, 1))
            tile = jnp.where(lane // 64 == c, tile, 0.0)
            charge_out[m, quarter, 0] = tile[:8]
            charge_out[m, quarter, 1] = tile[8:]
        mine = x * 2 + c
        for dx, dc in CROSS:
            to_x, to_c = (x + dx) % 4, (c + dc) % 2
            remote(
                charge_out.at[m, to_x, to_c], charge_in.at[m, mine], base + CHARGE, across(dx, dc)
            ).start()
        charge_in[m, mine] = charge_out[m, x, c]
        arrived(charge_in.at[m, pl.ds(0, 7)], base + CHARGE)
        block = jnp.concatenate(
            [charge_in[m, 2 * i] + charge_in[m, 2 * i + 1] for i in range(4)], axis=0
        ).astype(BF16)

        def block_at(line, row):
            columns = pl.ds(pl.multiple_of((line % 8) * 128, 128), 128)
            return gather_ref.at[m, row % 4, :, columns]

        block_at(z, y)[...] = block
        for dz in EIGHT:
            remote(block_at(z, y), block_at(z, y), base + LINE + dz, at(dz=dz)).start()
        for dy in FOUR:
            remote(block_at(z, y), block_at(z, y), base + PLANE + dy, at(dy=dy)).start()

        if m == 0:
            loads[L_NEAR].wait()
        arrived(ext_ref.at[m, pl.ds(0, 16)], base + NEAR)
        for b in range(8):
            total = jnp.zeros((16, 128), F32)
            for pair in range(4):
                sides = []
                for k in (2 * pair, 2 * pair + 1):
                    source = jnp.clip(ids_ref[b, k] - (s - 1) * 8, 0, 23)
                    live = (k < count_ref[b]).astype(F32)
                    sides.append((ext_ref[m, source].astype(F32) * live).astype(BF16))
                mats = jnp.concatenate([near_ref[b, 2 * pair], near_ref[b, 2 * pair + 1]], axis=1)
                total = total + dot_nt(jnp.concatenate(sides, axis=1), mats)
            columns = slice(128 * b, 128 * (b + 1))
            w_ref[:, columns] = total + self_ref[:, columns] * field[:, columns]

        for dz in EIGHT[::-1]:
            arrived(block_at(z - dz, y), base + LINE + dz)
            for dy in FOUR:
                remote(
                    block_at(z - dz, y), block_at(z - dz, y), base + PLANE + dy, at(dy=dy)
                ).start()

        if m == 0:
            arrived(couple_ref.at[oc], COUPLE)

        def multiply(row):
            return [dot_nt(gather_ref[m, row], couple_ref[side, row]) for side in range(2)]

        parts = multiply(y)
        for dy in FOUR[::-1]:
            arrived(gather_ref.at[m, (y + 4 - dy) % 4], base + PLANE + dy)
            parts = [a + b for a, b in zip(parts, multiply((y + 4 - dy) % 4))]
        for side in range(2):
            for i in range(4):
                far_out[m, side, i] = parts[side][8 * i : 8 * (i + 1)]
        for dx, dc in CROSS:
            to_x, to_c = (x + dx) % 4, (c + dc) % 2
            remote(
                far_out.at[m, to_c, to_x], far_in.at[m, mine], base + FAR, across(dx, dc)
            ).start()
        far_in[m, mine] = far_out[m, c, x]
        arrived(far_in.at[m, pl.ds(0, 7)], base + FAR)
        far = jnp.concatenate(
            [
                (far_in[m, i] + far_in[m, 2 + i]) + (far_in[m, 4 + i] + far_in[m, 6 + i])
                for i in range(2)
            ],
            axis=0,
        )
        results = []
        for half in range(2):
            part = far[:, 128 * half : 128 * (half + 1)]
            high, rest = halves(part)
            rest_high, rest_low = halves(part - high.astype(F32))
            stack = jnp.concatenate([high, rest_high, rest_low], axis=0)
            spread_out = dot_nn(stack, pick_ref[half]) + dot_nn(stack, put_ref[half])
            results.append(spread_out[:16] + spread_out[16:32] + spread_out[32:])
        return w_ref[...] + jnp.concatenate(results, axis=1)

    loads[L_RHS].wait()
    loads[L_U].wait()
    factor = u_ref[...]
    factor_high, factor_low = halves(factor)
    u_high[...] = factor_high
    u_low[...] = factor_low
    rhs = rhs_ref[...]
    partial = project(rhs)
    for index in (L_DIAG, L_SELF, L_INTERP, L_SKEL):
        loads[index].wait()

    pl.semaphore_wait(barrier, len(greeted))

    def start_rest():
        local(couple_ref.at[c], couple_ref.at[c], L_COUPLE).wait()
        remote(couple_ref.at[c], couple_ref.at[c], COUPLE, at(dc=1)).start()
        pick_ref[...] = jnp.zeros(pick_ref.shape, BF16)
        put_ref[...] = jnp.zeros(put_ref.shape, BF16)
        square = lax.broadcasted_iota(jnp.int32, (32, 32), 0)
        square = (square == lax.broadcasted_iota(jnp.int32, (32, 32), 1)).astype(F32)
        turned = dot_nt(square.astype(BF16), skel_ref[...].astype(F32).astype(BF16))
        panel = lax.broadcasted_iota(jnp.int32, (32, 128), 1).astype(F32)
        for b in range(8):
            rows = slice(32 * (b % 4), 32 * (b % 4 + 1))
            columns = slice(128 * (b % 4), 128 * (b % 4 + 1))
            chosen = (panel == turned[:, b : b + 1]).astype(F32)
            pick_ref[b // 4, rows, columns] = chosen.astype(BF16)
            put_ref[b // 4, rows, columns] = interp_ref[b]

    raw, total = all_reduce(0, partial, start_rest, row_of([lane_sum(rhs * rhs)]))
    beta_row = jnp.sqrt(total + EPS)
    beta = column_of(beta_row)
    first = rhs / beta
    first_coeffs = raw / beta
    diag = diag_ref[...]
    z_ref[0] = diag * first - expand(first_coeffs)
    norm_one = lane_sum(first * first)
    safe_one = jnp.where(norm_one > 1e-12, norm_one, 1.0)

    def along(inner, norm, safe):
        return jnp.where(norm > 1e-12, inner / safe, 0.0)

    residue = operate(0)

    def first_stats():
        own = along(lane_sum(residue * first), norm_one, safe_one)
        rest = residue - own * first
        send_stats(
            1, PHASES + STAT, [own, lane_sum(rest * first), norm_one, lane_sum(rest * rest)]
        )

    raw, _ = all_reduce(1, project(residue), first_stats)
    stats = read_stats(1, PHASES + STAT)

    def fields_of(stats, count):
        return [stats] + [pltpu.roll(stats, 128 - 16 * i, 1) for i in range(1, count)]

    def rows_sum(value):
        return jnp.sum(value, axis=0, keepdims=True)

    own, cross, norm, rest = fields_of(stats, 4)
    h11_row = rows_sum(cross + own * norm)
    shift = own - h11_row
    square = rows_sum(rest + 2.0 * shift * cross + shift * shift * norm)
    h21_row = jnp.sqrt(jnp.maximum(square, 0.0) + EPS)
    h11 = column_of(h11_row)
    h21 = column_of(h21_row)
    second = (residue - h11 * first) / h21
    second_coeffs = (raw - h11 * first_coeffs) / h21
    z_ref[1] = diag * second - expand(second_coeffs)
    norm_two = lane_sum(second * second)
    mixed = lane_sum(first * second)
    safe_two = jnp.where(norm_two > 1e-12, norm_two, 1.0)

    residue = operate(1)
    own_one = along(lane_sum(residue * first), norm_one, safe_one)
    rest = residue - own_one * first
    own_two = along(lane_sum(rest * second), norm_two, safe_two)
    rest = rest - own_two * second
    send_stats(
        2,
        FINAL,
        [
            own_one, own_two, lane_sum(rest * first), lane_sum(rest * second),
            norm_one, mixed, norm_two, lane_sum(rest * rest),
        ],
    )
    stats = read_stats(2, FINAL)
    own_one, own_two, cross_one, cross_two, n11, n12, n22, rest = fields_of(stats, 8)
    h12_row = rows_sum(cross_one + own_one * n11 + own_two * n12)
    h22_row = rows_sum(cross_two + own_one * n12 + own_two * n22)
    shift_one = own_one - h12_row
    shift_two = own_two - h22_row
    square = rows_sum(
        rest
        + 2.0 * (shift_one * cross_one + shift_two * cross_two)
        + shift_one * shift_one * n11
        + 2.0 * shift_one * shift_two * n12
        + shift_two * shift_two * n22
    )
    h32_row = jnp.sqrt(jnp.maximum(square, 0.0) + EPS)
    radius_one = jnp.sqrt(h11_row * h11_row + h21_row * h21_row)
    cos_one = h11_row / radius_one
    sin_one = h21_row / radius_one
    upper = cos_one * h12_row + sin_one * h22_row
    lower = cos_one * h22_row - sin_one * h12_row
    radius_two = jnp.sqrt(lower * lower + h32_row * h32_row)
    step_two = lower / radius_two * (-sin_one * beta_row) / radius_two
    step_one = (cos_one * beta_row - upper * step_two) / radius_one
    out_ref[...] = column_of(step_one) * z_ref[0] + column_of(step_two) * z_ref[1]

    sent(couple_ref.at[c], COUPLE)
    sent(stat_ref.at[1, pl.ds(0, 63), :], PHASES + STAT)
    sent(stat_ref.at[2, pl.ds(0, 63), :], FINAL)
    sent(line_ref.at[1], ROW_SIB)
    sent(line_ref.at[pl.ds(3, 3)], ROW_Y)
    sent(line_ref.at[pl.ds(7, 7)], ROW_Z)
    for m in range(2):
        base = m * PHASES
        sent(sib_ref.at[m], base + SIB)
        sent(y_ref.at[m, pl.ds(1, 3)], base + YAX)
        sent(zax_ref.at[m, pl.ds(1, 7)], base + ZAX)
        sent(full_ref.at[m, c], base + BACK)
        sent(ext_ref.at[m, pl.ds(0, 16)], base + NEAR)
        sent(charge_in.at[m, pl.ds(0, 7)], base + CHARGE)
        for dz in EIGHT:
            sent(gather_ref.at[m, 0, :, pl.ds(0, 128)], base + LINE + dz)
        for dy in FOUR:
            sent(gather_ref.at[m, 0], base + PLANE + dy)
        sent(far_in.at[m, pl.ds(0, 7)], base + FAR)


def on_device(
    rhs_vec, self_coef, near_mats, near_ids, near_count, interp, skel_idx, coupling,
    diag_prec, low_rank,
):
    anywhere = pl.BlockSpec(memory_space=pl.ANY)
    scalars = pl.BlockSpec(memory_space=pltpu.SMEM)
    vmem = pltpu.VMEM
    return pl.pallas_call(
        kernel,
        out_shape=jax.ShapeDtypeStruct((16, 1024), F32),
        in_specs=[
            anywhere, anywhere, anywhere, scalars, scalars, anywhere, anywhere, anywhere,
            anywhere, anywhere,
        ],
        out_specs=pl.BlockSpec(memory_space=pltpu.VMEM),
        scratch_shapes=[
            vmem((16, 1024), F32),
            vmem((1, 1024), F32),
            vmem((8, 8, 128, 128), BF16),
            vmem((8, 32, 128), BF16),
            vmem((8, 32), jnp.int32),
            vmem((2, 4, 256, 1024), BF16),
            vmem((1, 1024), F32),
            vmem((1024, 512), F32),
            vmem((1024, 512), BF16),
            vmem((1024, 512), BF16),
            vmem((2, 128, 512), BF16),
            vmem((2, 128, 512), BF16),
            vmem((2, 16, 1024), F32),
            vmem((16, 1024), F32),
            vmem((2, 2, 16, 256), F32),
            vmem((2, 16, 256), F32),
            vmem((2, 4, 16, 256), F32),
            vmem((2, 8, 16, 256), F32),
            vmem((2, 2, 16, 256), F32),
            vmem((14, 1, 128), F32),
            vmem((3, 1, 128), F32),
            vmem((3, 64, 128), F32),
            vmem((2, 24, 16, 128), BF16),
            vmem((2, 4, 2, 8, 128), F32),
            vmem((2, 8, 8, 128), F32),
            vmem((2, 4, 32, 1024), BF16),
            vmem((2, 2, 4, 8, 256), F32),
            vmem((2, 8, 8, 256), F32),
            pltpu.SemaphoreType.DMA((FINAL + 1,)),
            pltpu.SemaphoreType.DMA((FINAL + 1,)),
            pltpu.SemaphoreType.DMA((8,)),
        ],
        compiler_params=pltpu.CompilerParams(
            collective_id=0, has_side_effects=True, vmem_limit_bytes=56 * 1024 * 1024
        ),
        name="gmres",
    )(
        rhs_vec,
        self_coef.reshape(1, -1),
        near_mats,
        near_ids,
        near_count,
        jnp.swapaxes(interp, 1, 2),
        skel_idx,
        coupling.reshape(coupling.shape[0], coupling.shape[2]),
        diag_prec.reshape(1, -1),
        low_rank,
    )


def solution(mesh):
    placed = (
        P("rhs", "space"),
        P("space"),
        P("space", None, None, None),
        P("space", None),
        P("space"),
        P("space", None, None),
        P("space", None),
        P("space", "rhs", None),
        P("space"),
        P("space", None),
    )
    return jax.shard_map(
        on_device, mesh=mesh, in_specs=placed, out_specs=P("rhs", "space"), check_vma=False
    )
```

```python
import jax
import jax.numpy as jnp
from jax import lax
from jax.experimental import pallas as pl
from jax.experimental.pallas import tpu as pltpu
from jax.sharding import PartitionSpec as P

EPS = 1e-06
F32 = jnp.float32
BF16 = jnp.bfloat16
MESH = pl.DeviceIdType.MESH

(SIB, YAX, ZAX, BACK, STAT, NEAR, CHARGE, FAR, LINE) = range(9)
PLANE = LINE + 8
ROW_SIB = PLANE + 4
ROW_Y = ROW_SIB + 1
ROW_Z = ROW_SIB + 2
PHASES = ROW_SIB + 3
COUPLE = 2 * PHASES
FINAL = COUPLE + 1
FOUR = (2, 1, 3)
EIGHT = (4, 3, 5, 2, 6, 1, 7)
CROSS = ((2, 1), (2, 0), (1, 1), (3, 1), (1, 0), (3, 0), (0, 1))
(L_RHS, L_DIAG, L_SELF, L_INTERP, L_SKEL, L_NEAR, L_IDS, L_COUNT, L_COUPLE, L_U) = range(10)


def dot_nn(a, b):
    return lax.dot_general(a, b, (((1,), (0,)), ((), ())), preferred_element_type=F32)


def dot_nt(a, b):
    return lax.dot_general(a, b, (((1,), (1,)), ((), ())), preferred_element_type=F32)


def halves(value):
    high = value.astype(BF16)
    return high, (value - high.astype(F32)).astype(BF16)


def lane_sum(value):
    return jnp.sum(value, axis=1, keepdims=True)


def kernel(
    rhs_hbm, self_hbm, near_hbm, ids_hbm, count_hbm, interp_hbm, skel_hbm, couple_hbm,
    diag_hbm, u_hbm, out_ref,
    rhs_ref, self_ref, near_ref, ids_ref, count_ref, interp_ref, skel_ref, couple_ref, diag_ref, u_ref,
    u_high, u_low, pick_ref, put_ref, z_ref, w_ref,
    part_ref, sib_ref, y_ref, zax_ref, full_ref, line_ref, row_ref, stat_ref,
    ext_ref, charge_out, charge_in, gather_ref, far_out, far_in,
    send_sems, recv_sems, local_sems,
):
    s = lax.axis_index("space")
    x = lax.axis_index("rhs")
    z = s // 8
    y = (s // 2) % 4
    c = s % 2
    oc = 1 - c
    chip = s // 2
    sibling = (chip * 2 + oc, x)

    def local(src, dst, index):
        return pltpu.make_async_copy(src, dst, local_sems.at[index])

    def factor_rows(part):
        return pl.ds(256 * part, 256)

    factor_loads = [
        local(u_hbm.at[factor_rows(part)], u_ref.at[factor_rows(part)], L_U + part)
        for part in range(4)
    ]
    loads = [
        local(rhs_hbm, rhs_ref, L_RHS),
        local(diag_hbm, diag_ref, L_DIAG),
        local(self_hbm, self_ref, L_SELF),
        local(interp_hbm, interp_ref, L_INTERP),
        local(skel_hbm, skel_ref, L_SKEL),
        local(near_hbm, near_ref, L_NEAR),
        local(ids_hbm, ids_ref, L_IDS),
        local(count_hbm, count_ref, L_COUNT),
    ]
    loads[L_RHS].start()
    for load in factor_loads:
        load.start()

    barrier = pltpu.get_barrier_semaphore()

    def at(dz=0, dy=0, dc=0):
        return ((((z + dz) % 8) * 4 + (y + dy) % 4) * 2 + (c + dc) % 2, x)

    def across(dx, dc):
        return (chip * 2 + (c + dc) % 2, (x + dx) % 4)

    greeted = [at(dz=dz) for dz in EIGHT] + [at(dy=dy) for dy in FOUR]
    greeted += [across(dx, dc) for dx, dc in CROSS]
    for device in greeted:
        pl.semaphore_signal(barrier, inc=1, device_id=device, device_id_type=MESH)

    def remote(src, dst, phase, device):
        return pltpu.make_async_remote_copy(
            src_ref=src,
            dst_ref=dst,
            send_sem=send_sems.at[phase],
            recv_sem=recv_sems.at[phase],
            device_id=device,
            device_id_type=MESH,
        )

    def arrived(ref, phase):
        remote(ref, ref, phase, sibling).wait_recv()

    def sent(ref, phase):
        remote(ref, ref, phase, sibling).wait_send()

    lane = lax.broadcasted_iota(jnp.int32, (16, 128), 1)
    excitation = lax.broadcasted_iota(jnp.int32, (16, 128), 0)

    def row_of(fields):
        total = jnp.zeros((16, 128), F32)
        for index, field in enumerate(fields):
            total = total + jnp.where(lane == index * 16 + excitation, field, 0.0)
        return jnp.sum(total, axis=0, keepdims=True)

    def column_of(row):
        return lane_sum(jnp.where(lane == excitation, row, 0.0))

    def project(value):
        high, low = halves(value)
        both = dot_nn(jnp.concatenate([high, low], axis=0), u_high[...])
        return both[:16] + both[16:] + dot_nn(high, u_low[...])

    def expand(coeffs):
        high, low = halves(coeffs)
        both = dot_nt(jnp.concatenate([high, low], axis=0), u_high[...])
        return both[:16] + both[16:] + dot_nt(high, u_low[...])

    def send_stats(index, phase, fields):
        row_ref[index] = row_of(fields)
        stat_ref[index, pl.ds(s, 1), :] = row_ref[index]

        def tell(step, carry):
            dz = (4 + (step % 2 * -2 + 1) * ((step + 1) // 2)) % 8
            for dy in (2, 1, 3):
                for dc in (1, 0):
                    remote(
                        row_ref.at[index], stat_ref.at[index, pl.ds(s, 1), :], phase,
                        at(dz, dy, dc),
                    ).start()
            remote(
                row_ref.at[index], stat_ref.at[index, pl.ds(s, 1), :], phase, at(dz, 0, 1)
            ).start()
            return carry

        lax.fori_loop(0, 8, tell, 0)
        for dz in EIGHT:
            remote(
                row_ref.at[index], stat_ref.at[index, pl.ds(s, 1), :], phase, at(dz)
            ).start()

    def read_stats(index, phase):
        arrived(stat_ref.at[index, pl.ds(0, 63), :], phase)
        return stat_ref[index]

    def all_reduce(m, partial, between, row=None, later=None):
        base = m * PHASES
        part_ref[m, 0] = partial[:, :256]
        part_ref[m, 1] = partial[:, 256:]
        remote(part_ref.at[m, oc], sib_ref.at[m], base + SIB, at(dc=1)).start()
        if row is not None:
            line_ref[0] = row
            remote(line_ref.at[0], line_ref.at[1], base + ROW_SIB, at(dc=1)).start()
        arrived(sib_ref.at[m], base + SIB)
        y_ref[m, 0] = part_ref[m, c] + sib_ref[m]
        for dy in FOUR:
            remote(y_ref.at[m, 0], y_ref.at[m, dy], base + YAX, at(dy=dy)).start()
        if row is not None:
            arrived(line_ref.at[1], base + ROW_SIB)
            line_ref[2] = line_ref[0] + line_ref[1]
            for dy in FOUR:
                remote(line_ref.at[2], line_ref.at[2 + dy], base + ROW_Y, at(dy=dy)).start()
        between()
        arrived(y_ref.at[m, pl.ds(1, 3)], base + YAX)
        zax_ref[m, 0] = (y_ref[m, 0] + y_ref[m, 1]) + (y_ref[m, 2] + y_ref[m, 3])
        for dz in EIGHT:
            remote(zax_ref.at[m, 0], zax_ref.at[m, dz], base + ZAX, at(dz=dz)).start()
        if row is not None:
            later()
            arrived(line_ref.at[pl.ds(3, 3)], base + ROW_Y)
            line_ref[6] = (line_ref[2] + line_ref[3]) + (line_ref[4] + line_ref[5])
            for dz in EIGHT:
                remote(line_ref.at[6], line_ref.at[6 + dz], base + ROW_Z, at(dz=dz)).start()
        arrived(zax_ref.at[m, pl.ds(1, 7)], base + ZAX)
        pairs = [zax_ref[m, 2 * i] + zax_ref[m, 2 * i + 1] for i in range(4)]
        full_ref[m, c] = (pairs[0] + pairs[1]) + (pairs[2] + pairs[3])
        remote(full_ref.at[m, c], full_ref.at[m, c], base + BACK, at(dc=1)).start()
        if row is not None:
            arrived(line_ref.at[pl.ds(7, 7)], base + ROW_Z)
            pairs = [line_ref[6 + 2 * i] + line_ref[7 + 2 * i] for i in range(4)]
            row = (pairs[0] + pairs[1]) + (pairs[2] + pairs[3])
        arrived(full_ref.at[m, oc], base + BACK)
        return jnp.concatenate([full_ref[m, 0], full_ref[m, 1]], axis=1), row

    def operate(m):
        base = m * PHASES
        field = z_ref[m]
        low = field.astype(BF16)
        for b in range(8):
            ext_ref[m, 8 + b] = low[:, 128 * b : 128 * (b + 1)]
        remote(
            ext_ref.at[m, pl.ds(8, 8)], ext_ref.at[m, pl.ds(0, 8)], base + NEAR, ((s + 1) % 64, x)
        ).start()
        remote(
            ext_ref.at[m, pl.ds(8, 8)], ext_ref.at[m, pl.ds(16, 8)], base + NEAR, ((s + 63) % 64, x)
        ).start()
        charges = []
        for half in range(2):
            part = low[:, 512 * half : 512 * (half + 1)]
            charges.append(dot_nt(part, pick_ref[half]) + dot_nt(part, put_ref[half]))
        for quarter in range(4):
            tile = charges[quarter // 2]
            tile = jnp.where(c == quarter % 2, tile, pltpu.roll(tile, 64, 1))
            tile = jnp.where(lane // 64 == c, tile, 0.0)
            charge_out[m, quarter, 0] = tile[:8]
            charge_out[m, quarter, 1] = tile[8:]
        mine = x * 2 + c
        for dx, dc in CROSS:
            to_x, to_c = (x + dx) % 4, (c + dc) % 2
            remote(
                charge_out.at[m, to_x, to_c], charge_in.at[m, mine], base + CHARGE, across(dx, dc)
            ).start()
        charge_in[m, mine] = charge_out[m, x, c]
        arrived(charge_in.at[m, pl.ds(0, 7)], base + CHARGE)
        block = jnp.concatenate(
            [charge_in[m, 2 * i] + charge_in[m, 2 * i + 1] for i in range(4)], axis=0
        ).astype(BF16)

        def block_at(line, row):
            columns = pl.ds(pl.multiple_of((line % 8) * 128, 128), 128)
            return gather_ref.at[m, row % 4, :, columns]

        block_at(z, y)[...] = block
        for dz in EIGHT:
            remote(block_at(z, y), block_at(z, y), base + LINE + dz, at(dz=dz)).start()
        for dy in FOUR:
            remote(block_at(z, y), block_at(z, y), base + PLANE + dy, at(dy=dy)).start()

        if m == 0:
            for index in (L_NEAR, L_IDS, L_COUNT):
                loads[index].wait()
        arrived(ext_ref.at[m, pl.ds(0, 16)], base + NEAR)
        for b in range(8):
            total = jnp.zeros((16, 128), F32)
            for pair in range(4):
                sides = []
                for k in (2 * pair, 2 * pair + 1):
                    source = jnp.clip(ids_ref[b, k] - (s - 1) * 8, 0, 23)
                    live = (k < count_ref[b]).astype(F32)
                    sides.append((ext_ref[m, source].astype(F32) * live).astype(BF16))
                mats = jnp.concatenate([near_ref[b, 2 * pair], near_ref[b, 2 * pair + 1]], axis=1)
                total = total + dot_nt(jnp.concatenate(sides, axis=1), mats)
            columns = slice(128 * b, 128 * (b + 1))
            w_ref[:, columns] = total + self_ref[:, columns] * field[:, columns]

        for dz in EIGHT[::-1]:
            arrived(block_at(z - dz, y), base + LINE + dz)
            for dy in FOUR:
                remote(
                    block_at(z - dz, y), block_at(z - dz, y), base + PLANE + dy, at(dy=dy)
                ).start()

        if m == 0:
            arrived(couple_ref.at[oc], COUPLE)

        def multiply(row):
            return [dot_nt(gather_ref[m, row], couple_ref[side, row]) for side in range(2)]

        parts = multiply(y)
        for dy in FOUR[::-1]:
            arrived(gather_ref.at[m, (y + 4 - dy) % 4], base + PLANE + dy)
            parts = [a + b for a, b in zip(parts, multiply((y + 4 - dy) % 4))]
        for side in range(2):
            for i in range(4):
                far_out[m, side, i] = parts[side][8 * i : 8 * (i + 1)]
        for dx, dc in CROSS:
            to_x, to_c = (x + dx) % 4, (c + dc) % 2
            remote(
                far_out.at[m, to_c, to_x], far_in.at[m, mine], base + FAR, across(dx, dc)
            ).start()
        far_in[m, mine] = far_out[m, c, x]
        arrived(far_in.at[m, pl.ds(0, 7)], base + FAR)
        far = jnp.concatenate(
            [
                (far_in[m, i] + far_in[m, 2 + i]) + (far_in[m, 4 + i] + far_in[m, 6 + i])
                for i in range(2)
            ],
            axis=0,
        )
        results = []
        for half in range(2):
            part = far[:, 128 * half : 128 * (half + 1)]
            high, rest = halves(part)
            rest_high, rest_low = halves(part - high.astype(F32))
            stack = jnp.concatenate([high, rest_high, rest_low], axis=0)
            spread_out = dot_nn(stack, pick_ref[half]) + dot_nn(stack, put_ref[half])
            results.append(spread_out[:16] + spread_out[16:32] + spread_out[32:])
        return w_ref[...] + jnp.concatenate(results, axis=1)

    loads[L_RHS].wait()
    rhs = rhs_ref[...]
    rhs_high, rhs_low = halves(rhs)
    partial = jnp.zeros((16, 512), F32)
    for part in range(4):
        rows, columns = slice(256 * part, 256 * (part + 1)), slice(256 * part, 256 * (part + 1))
        factor_loads[part].wait()
        factor_high, factor_low = halves(u_ref[rows, :])
        u_high[rows, :] = factor_high
        u_low[rows, :] = factor_low
        high, low = rhs_high[:, columns], rhs_low[:, columns]
        both = dot_nn(jnp.concatenate([high, low], axis=0), factor_high)
        partial = partial + (both[:16] + both[16:] + dot_nn(high, factor_low))

    for load in loads[1:]:
        load.start()

    def load_columns(line, carry):
        for row in range(4):
            source = pl.multiple_of((line * 4 + row) * 128, 128)
            local(
                couple_hbm.at[:, pl.ds(source, 128)],
                couple_ref.at[c, row, :, pl.ds(pl.multiple_of(line * 128, 128), 128)],
                L_COUPLE,
            ).start()
        return carry

    lax.fori_loop(0, 8, load_columns, 0)

    pl.semaphore_wait(barrier, len(greeted))

    def share_coupling():
        local(couple_ref.at[c], couple_ref.at[c], L_COUPLE).wait()
        remote(couple_ref.at[c], couple_ref.at[c], COUPLE, at(dc=1)).start()

    def start_rest():
        for index in (L_DIAG, L_SELF, L_INTERP, L_SKEL):
            loads[index].wait()
        pick_ref[...] = jnp.zeros(pick_ref.shape, BF16)
        put_ref[...] = jnp.zeros(put_ref.shape, BF16)
        square = lax.broadcasted_iota(jnp.int32, (32, 32), 0)
        square = (square == lax.broadcasted_iota(jnp.int32, (32, 32), 1)).astype(F32)
        turned = dot_nt(square.astype(BF16), skel_ref[...].astype(F32).astype(BF16))
        panel = lax.broadcasted_iota(jnp.int32, (32, 128), 1).astype(F32)
        for b in range(8):
            rows = slice(32 * (b % 4), 32 * (b % 4 + 1))
            columns = slice(128 * (b % 4), 128 * (b % 4 + 1))
            chosen = (panel == turned[:, b : b + 1]).astype(F32)
            pick_ref[b // 4, rows, columns] = chosen.astype(BF16)
            put_ref[b // 4, rows, columns] = interp_ref[b]

    raw, total = all_reduce(
        0, partial, start_rest, row_of([lane_sum(rhs * rhs)]), share_coupling
    )
    beta_row = jnp.sqrt(total + EPS)
    beta = column_of(beta_row)
    first = rhs / beta
    first_coeffs = raw / beta
    diag = diag_ref[...]
    z_ref[0] = diag * first - expand(first_coeffs)
    norm_one = lane_sum(first * first)
    safe_one = jnp.where(norm_one > 1e-12, norm_one, 1.0)

    def along(inner, norm, safe):
        return jnp.where(norm > 1e-12, inner / safe, 0.0)

    residue = operate(0)

    def first_stats():
        own = along(lane_sum(residue * first), norm_one, safe_one)
        rest = residue - own * first
        send_stats(
            1, PHASES + STAT, [own, lane_sum(rest * first), norm_one, lane_sum(rest * rest)]
        )

    raw, _ = all_reduce(1, project(residue), first_stats)
    stats = read_stats(1, PHASES + STAT)

    def fields_of(stats, count):
        return [stats] + [pltpu.roll(stats, 128 - 16 * i, 1) for i in range(1, count)]

    def rows_sum(value):
        return jnp.sum(value, axis=0, keepdims=True)

    own, cross, norm, rest = fields_of(stats, 4)
    h11_row = rows_sum(cross + own * norm)
    shift = own - h11_row
    square = rows_sum(rest + 2.0 * shift * cross + shift * shift * norm)
    h21_row = jnp.sqrt(jnp.maximum(square, 0.0) + EPS)
    h11 = column_of(h11_row)
    h21 = column_of(h21_row)
    second = (residue - h11 * first) / h21
    second_coeffs = (raw - h11 * first_coeffs) / h21
    z_ref[1] = diag * second - expand(second_coeffs)
    norm_two = lane_sum(second * second)
    mixed = lane_sum(first * second)
    safe_two = jnp.where(norm_two > 1e-12, norm_two, 1.0)

    residue = operate(1)
    own_one = along(lane_sum(residue * first), norm_one, safe_one)
    rest = residue - own_one * first
    own_two = along(lane_sum(rest * second), norm_two, safe_two)
    rest = rest - own_two * second
    send_stats(
        2,
        FINAL,
        [
            own_one, own_two, lane_sum(rest * first), lane_sum(rest * second),
            norm_one, mixed, norm_two, lane_sum(rest * rest),
        ],
    )
    stats = read_stats(2, FINAL)
    own_one, own_two, cross_one, cross_two, n11, n12, n22, rest = fields_of(stats, 8)
    h12_row = rows_sum(cross_one + own_one * n11 + own_two * n12)
    h22_row = rows_sum(cross_two + own_one * n12 + own_two * n22)
    shift_one = own_one - h12_row
    shift_two = own_two - h22_row
    square = rows_sum(
        rest
        + 2.0 * (shift_one * cross_one + shift_two * cross_two)
        + shift_one * shift_one * n11
        + 2.0 * shift_one * shift_two * n12
        + shift_two * shift_two * n22
    )
    h32_row = jnp.sqrt(jnp.maximum(square, 0.0) + EPS)
    radius_one = jnp.sqrt(h11_row * h11_row + h21_row * h21_row)
    cos_one = h11_row / radius_one
    sin_one = h21_row / radius_one
    upper = cos_one * h12_row + sin_one * h22_row
    lower = cos_one * h22_row - sin_one * h12_row
    radius_two = jnp.sqrt(lower * lower + h32_row * h32_row)
    step_two = lower / radius_two * (-sin_one * beta_row) / radius_two
    step_one = (cos_one * beta_row - upper * step_two) / radius_one
    out_ref[...] = column_of(step_one) * z_ref[0] + column_of(step_two) * z_ref[1]

    sent(couple_ref.at[c], COUPLE)
    sent(stat_ref.at[1, pl.ds(0, 63), :], PHASES + STAT)
    sent(stat_ref.at[2, pl.ds(0, 63), :], FINAL)
    sent(line_ref.at[1], ROW_SIB)
    sent(line_ref.at[pl.ds(3, 3)], ROW_Y)
    sent(line_ref.at[pl.ds(7, 7)], ROW_Z)
    for m in range(2):
        base = m * PHASES
        sent(sib_ref.at[m], base + SIB)
        sent(y_ref.at[m, pl.ds(1, 3)], base + YAX)
        sent(zax_ref.at[m, pl.ds(1, 7)], base + ZAX)
        sent(full_ref.at[m, c], base + BACK)
        sent(ext_ref.at[m, pl.ds(0, 16)], base + NEAR)
        sent(charge_in.at[m, pl.ds(0, 7)], base + CHARGE)
        for dz in EIGHT:
            sent(gather_ref.at[m, 0, :, pl.ds(0, 128)], base + LINE + dz)
        for dy in FOUR:
            sent(gather_ref.at[m, 0], base + PLANE + dy)
        sent(far_in.at[m, pl.ds(0, 7)], base + FAR)


def hbm(value):
    return pltpu.with_memory_space_constraint(value, pltpu.HBM)


def on_device(
    rhs_vec, self_coef, near_mats, near_ids, near_count, interp, skel_idx, coupling,
    diag_prec, low_rank,
):
    vmem = pltpu.VMEM
    return pl.pallas_call(
        kernel,
        out_shape=jax.ShapeDtypeStruct((16, 1024), F32),
        in_specs=[pl.BlockSpec(memory_space=pltpu.HBM)] * 10,
        out_specs=pl.BlockSpec(memory_space=pltpu.VMEM),
        scratch_shapes=[
            vmem((16, 1024), F32),
            vmem((1, 1024), F32),
            vmem((8, 8, 128, 128), BF16),
            pltpu.SMEM((8, 8), jnp.int32),
            pltpu.SMEM((8,), jnp.int32),
            vmem((8, 32, 128), BF16),
            vmem((8, 32), jnp.int32),
            vmem((2, 4, 256, 1024), BF16),
            vmem((1, 1024), F32),
            vmem((1024, 512), F32),
            vmem((1024, 512), BF16),
            vmem((1024, 512), BF16),
            vmem((2, 128, 512), BF16),
            vmem((2, 128, 512), BF16),
            vmem((2, 16, 1024), F32),
            vmem((16, 1024), F32),
            vmem((2, 2, 16, 256), F32),
            vmem((2, 16, 256), F32),
            vmem((2, 4, 16, 256), F32),
            vmem((2, 8, 16, 256), F32),
            vmem((2, 2, 16, 256), F32),
            vmem((14, 1, 128), F32),
            vmem((3, 1, 128), F32),
            vmem((3, 64, 128), F32),
            vmem((2, 24, 16, 128), BF16),
            vmem((2, 4, 2, 8, 128), F32),
            vmem((2, 8, 8, 128), F32),
            vmem((2, 4, 32, 1024), BF16),
            vmem((2, 2, 4, 8, 256), F32),
            vmem((2, 8, 8, 256), F32),
            pltpu.SemaphoreType.DMA((FINAL + 1,)),
            pltpu.SemaphoreType.DMA((FINAL + 1,)),
            pltpu.SemaphoreType.DMA((L_U + 4,)),
        ],
        compiler_params=pltpu.CompilerParams(
            collective_id=0, has_side_effects=True, vmem_limit_bytes=24 * 1024 * 1024
        ),
        name="gmres",
    )(
        hbm(rhs_vec),
        hbm(self_coef.reshape(1, -1)),
        hbm(near_mats),
        hbm(near_ids),
        hbm(near_count),
        hbm(jnp.swapaxes(interp, 1, 2)),
        hbm(skel_idx),
        hbm(coupling.reshape(coupling.shape[0], coupling.shape[2])),
        hbm(diag_prec.reshape(1, -1)),
        hbm(low_rank),
    )


def solution(mesh):
    placed = (
        P("rhs", "space"),
        P("space"),
        P("space", None, None, None),
        P("space", None),
        P("space"),
        P("space", None, None),
        P("space", None),
        P("space", "rhs", None),
        P("space"),
        P("space", None),
    )
    return jax.shard_map(
        on_device, mesh=mesh, in_specs=placed, out_specs=P("rhs", "space"), check_vma=False
    )
```

```python
import jax
import jax.numpy as jnp
from jax import lax
from jax.experimental import pallas as pl
from jax.experimental.pallas import tpu as pltpu
from jax.sharding import PartitionSpec as P

EPS = 1e-06
F32 = jnp.float32
BF16 = jnp.bfloat16
MESH = pl.DeviceIdType.MESH

(YAX, ZAX, ROW_Y, ROW_Z, STAT, NEAR, NEAR_BACK, CHARGE, FAR, LINE) = range(10)
PLANE = LINE + 8
PHASES = PLANE + 4
(PART, RHS, DIAG, SELF, PICK, PUT, HIGH, LOW, COUPLE, FINAL, RESULT) = range(2 * PHASES, 2 * PHASES + 11)
FOUR = (2, 1, 3)
EIGHT = (4, 3, 5, 2, 6, 1, 7)
(L_RHS, L_DIAG, L_SELF, L_INTERP, L_SKEL, L_NEAR, L_IDS, L_COUNT, L_COUPLE, L_U) = range(10)


def dot_nn(a, b):
    return lax.dot_general(a, b, (((1,), (0,)), ((), ())), preferred_element_type=F32)


def dot_nt(a, b):
    return lax.dot_general(a, b, (((1,), (1,)), ((), ())), preferred_element_type=F32)


def halves(value):
    high = value.astype(BF16)
    return high, (value - high.astype(F32)).astype(BF16)


def stacked(pieces):
    return jnp.concatenate([piece.astype(F32) for piece in pieces], axis=0).astype(BF16)


def lane_sum(value):
    return jnp.sum(value, axis=1, keepdims=True)


def kernel(
    rhs_hbm, self_hbm, near_hbm, ids_hbm, count_hbm, interp_hbm, skel_hbm, couple_hbm,
    diag_hbm, u_hbm, out_ref,
    rhs_ref, self_ref, near_ref, ids_ref, count_ref, interp_ref, skel_ref, couple_ref, diag_ref,
    u_ref, u_high, u_low, pick_ref, put_ref, z_ref, w_ref,
    part_ref, sib_ref, both_ref, y_ref, zax_ref, line_ref, row_ref, stat_ref,
    blocks_ref, ext_ref, near_out, near_in, charge_out, charge_in, gather_ref, far_out, far_in,
    result_ref, other_ref,
    send_sems, recv_sems, local_sems,
):
    s = lax.axis_index("space")
    x = lax.axis_index("rhs")
    z = s // 8
    y = (s // 2) % 4
    c = s % 2
    oc = 1 - c
    chip = s // 2
    sibling = (chip * 2 + oc, x)

    def local(src, dst, index):
        return pltpu.make_async_copy(src, dst, local_sems.at[index])

    def factor_rows(part):
        return pl.ds(256 * part, 256)

    factor_loads = [
        local(u_hbm.at[factor_rows(part)], u_ref.at[factor_rows(part)], L_U + part)
        for part in range(4)
    ]
    loads = [
        local(rhs_hbm, rhs_ref, L_RHS),
        local(diag_hbm, diag_ref.at[c], L_DIAG),
        local(self_hbm, self_ref.at[c], L_SELF),
        local(interp_hbm, interp_ref, L_INTERP),
        local(skel_hbm, skel_ref, L_SKEL),
        local(near_hbm, near_ref, L_NEAR),
        local(ids_hbm, ids_ref, L_IDS),
        local(count_hbm, count_ref, L_COUNT),
    ]
    loads[L_RHS].start()
    for load in factor_loads:
        load.start()

    def at(dz=0, dy=0):
        return ((((z + dz) % 8) * 4 + (y + dy) % 4) * 2 + c, x)

    def across(dx):
        return (s, (x + dx) % 4)

    barrier = pltpu.get_barrier_semaphore()
    greeted = [sibling] + [at(dz=dz) for dz in EIGHT] + [at(dy=dy) for dy in FOUR]
    greeted += [across(dx) for dx in FOUR]
    for device in greeted:
        pl.semaphore_signal(barrier, inc=1, device_id=device, device_id_type=MESH)

    def remote(src, dst, phase, device):
        return pltpu.make_async_remote_copy(
            src_ref=src,
            dst_ref=dst,
            send_sem=send_sems.at[phase],
            recv_sem=recv_sems.at[phase],
            device_id=device,
            device_id_type=MESH,
        )

    def arrived(ref, phase):
        remote(ref, ref, phase, sibling).wait_recv()

    def sent(ref, phase):
        remote(ref, ref, phase, sibling).wait_send()

    lane = lax.broadcasted_iota(jnp.int32, (8, 128), 1)
    excitation = lax.broadcasted_iota(jnp.int32, (8, 128), 0)

    def row_of(fields):
        total = jnp.zeros((8, 128), F32)
        for index, field in enumerate(fields):
            total = total + jnp.where(lane == index * 8 + excitation, field, 0.0)
        return jnp.sum(total, axis=0, keepdims=True)

    def column_of(row):
        return lane_sum(jnp.where(lane == excitation, row, 0.0))

    def project(value):
        high, low = halves(value)
        both = jnp.zeros((16, 512), F32)
        rest = jnp.zeros((8, 512), F32)
        stack = stacked([high, low])
        for region in range(2):
            columns = slice(1024 * region, 1024 * (region + 1))
            both = both + dot_nn(stack[:, columns], u_high[region])
            rest = rest + dot_nn(high[:, columns], u_low[region])
        return both[:8] + both[8:] + rest

    def expand(coeffs):
        high, low = halves(coeffs)
        stack = stacked([high, low])
        results = []
        for region in range(2):
            both = dot_nt(stack, u_high[region])
            results.append(both[:8] + both[8:] + dot_nt(high, u_low[region]))
        return jnp.concatenate(results, axis=1)

    def send_stats(index, phase, fields):
        row_ref[index] = row_of(fields)
        stat_ref[index, pl.ds(chip, 1), :] = row_ref[index]
        for dz in EIGHT + (0,):
            for dy in FOUR + (0,):
                if dz or dy:
                    remote(
                        row_ref.at[index], stat_ref.at[index, pl.ds(chip, 1), :], phase, at(dz, dy)
                    ).start()

    def read_stats(index, phase):
        arrived(stat_ref.at[index, pl.ds(0, 31), :], phase)
        return stat_ref[index]

    def all_reduce(m, partial, between, row=None, later=None):
        base = m * PHASES
        y_ref[m, 0] = partial
        for dy in FOUR:
            remote(y_ref.at[m, 0], y_ref.at[m, dy], base + YAX, at(dy=dy)).start()
        if row is not None:
            line_ref[0] = row
            for dy in FOUR:
                remote(line_ref.at[0], line_ref.at[dy], base + ROW_Y, at(dy=dy)).start()
        between()
        arrived(y_ref.at[m, pl.ds(1, 3)], base + YAX)
        zax_ref[m, 0] = (y_ref[m, 0] + y_ref[m, 1]) + (y_ref[m, 2] + y_ref[m, 3])
        for dz in EIGHT:
            remote(zax_ref.at[m, 0], zax_ref.at[m, dz], base + ZAX, at(dz=dz)).start()
        if row is not None:
            arrived(line_ref.at[pl.ds(1, 3)], base + ROW_Y)
            line_ref[4] = (line_ref[0] + line_ref[1]) + (line_ref[2] + line_ref[3])
            for dz in EIGHT:
                remote(line_ref.at[4], line_ref.at[4 + dz], base + ROW_Z, at(dz=dz)).start()
            later()
            arrived(line_ref.at[pl.ds(5, 7)], base + ROW_Z)
            pairs = [line_ref[4 + 2 * i] + line_ref[5 + 2 * i] for i in range(4)]
            row = (pairs[0] + pairs[1]) + (pairs[2] + pairs[3])
        arrived(zax_ref.at[m, pl.ds(1, 7)], base + ZAX)
        pairs = [zax_ref[m, 2 * i] + zax_ref[m, 2 * i + 1] for i in range(4)]
        return (pairs[0] + pairs[1]) + (pairs[2] + pairs[3]), row

    def operate(m):
        base = m * PHASES
        field = z_ref[m]
        low = field.astype(BF16)
        charges = []
        for region in range(2):
            for half in range(2):
                start = 1024 * region + 512 * half
                part = low[:, start : start + 512]
                charges.append(
                    dot_nt(part, pick_ref[region, half]) + dot_nt(part, put_ref[region, half])
                )
        for quarter in range(4):
            first_region, second_region = charges[quarter // 2], charges[2 + quarter // 2]
            if quarter % 2:
                first_region = pltpu.roll(first_region, 64, 1)
            else:
                second_region = pltpu.roll(second_region, 64, 1)
            charge_out[m, quarter] = jnp.where(lane < 64, first_region, second_region)
        for dx in FOUR:
            remote(
                charge_out.at[m, (x + dx) % 4], charge_in.at[m, x], base + CHARGE, across(dx)
            ).start()
        charge_in[m, x] = charge_out[m, x]

        for i in range(16):
            block = field[:, 128 * i : 128 * (i + 1)]
            blocks_ref[m, i] = block
            ext_ref[m, 8 * oc + i, c] = block
        remote(
            blocks_ref.at[m], ext_ref.at[m, pl.ds(8 * c, 16), c], base + NEAR, sibling
        ).start()
        remote(
            blocks_ref.at[m, pl.ds(0, 8)],
            ext_ref.at[m, pl.ds(16, 8), c],
            base + NEAR,
            (((chip + 31) % 32) * 2 + 1, x),
        ).start()
        remote(
            blocks_ref.at[m, pl.ds(8, 8)],
            ext_ref.at[m, pl.ds(0, 8), c],
            base + NEAR,
            (((chip + 1) % 32) * 2, x),
        ).start()

        arrived(charge_in.at[m, pl.ds(0, 3)], base + CHARGE)
        block = jnp.concatenate([charge_in[m, i] for i in range(4)], axis=0).astype(BF16)

        def block_at(line, row):
            columns = pl.ds(pl.multiple_of((line % 8) * 128, 128), 128)
            return gather_ref.at[m, row % 4, :, columns]

        block_at(z, y)[...] = block
        for dz in EIGHT:
            remote(block_at(z, y), block_at(z, y), base + LINE + dz, at(dz=dz)).start()
        for dy in FOUR:
            remote(block_at(z, y), block_at(z, y), base + PLANE + dy, at(dy=dy)).start()

        if m == 0:
            for index in (L_NEAR, L_IDS, L_COUNT):
                loads[index].wait()
        arrived(ext_ref.at[m, pl.ds(0, 16)], base + NEAR)
        for b in range(8):
            total = jnp.zeros((16, 128), F32)
            for pair in range(4):
                sides = []
                for k in (2 * pair, 2 * pair + 1):
                    source = jnp.clip(ids_ref[b, k] - (s - 1) * 8, 0, 23)
                    live = (k < count_ref[b]).astype(F32)
                    found = ext_ref[m, source].reshape(16, 128)
                    sides.append((found * live).astype(BF16))
                mats = jnp.concatenate([near_ref[b, 2 * pair], near_ref[b, 2 * pair + 1]], axis=1)
                total = total + dot_nt(jnp.concatenate(sides, axis=1), mats)
            near_out[m, 0, b] = total[:8]
            near_out[m, 1, b] = total[8:]
        remote(near_out.at[m, oc], near_in.at[m, c], base + NEAR_BACK, sibling).start()

        for dz in EIGHT[::-1]:
            arrived(block_at(z - dz, y), base + LINE + dz)
            for dy in FOUR:
                remote(
                    block_at(z - dz, y), block_at(z - dz, y), base + PLANE + dy, at(dy=dy)
                ).start()

        if m == 0:
            arrived(couple_ref.at[oc], COUPLE)

        def multiply(row):
            return [dot_nt(gather_ref[m, row], couple_ref[side, row]) for side in range(2)]

        parts = multiply(y)
        near_in[m, c] = near_out[m, c]
        arrived(near_in.at[m, oc], base + NEAR_BACK)
        for region in range(2):
            for b in range(8):
                start = 1024 * region + 128 * b
                columns = slice(start, start + 128)
                own_coef = self_ref[region, :, 128 * b : 128 * (b + 1)]
                w_ref[:, columns] = own_coef * field[:, columns] + near_in[m, region, b]
        for dy in FOUR[::-1]:
            arrived(gather_ref.at[m, (y + 4 - dy) % 4], base + PLANE + dy)
            parts = [a + b for a, b in zip(parts, multiply((y + 4 - dy) % 4))]
        for i in range(4):
            for side in range(2):
                far_out[m, i, side] = parts[side][8 * i : 8 * (i + 1)]
        for dx in FOUR:
            remote(far_out.at[m, (x + dx) % 4], far_in.at[m, x], base + FAR, across(dx)).start()
        far_in[m, x] = far_out[m, x]
        arrived(far_in.at[m, pl.ds(0, 3)], base + FAR)
        results = []
        for side in range(2):
            far = (far_in[m, 0, side] + far_in[m, 1, side]) + (
                far_in[m, 2, side] + far_in[m, 3, side]
            )
            for half in range(2):
                part = far[:, 128 * half : 128 * (half + 1)]
                high, _ = halves(part)
                rest_high, rest_low = halves(part - high.astype(F32))
                stack = stacked([high, rest_high, rest_low])
                spread_out = dot_nn(stack, pick_ref[side, half]) + dot_nn(stack, put_ref[side, half])
                results.append(spread_out[:8] + spread_out[8:16] + spread_out[16:])
        return w_ref[...] + jnp.concatenate(results, axis=1)

    loads[L_RHS].wait()
    rhs_high, rhs_low = halves(rhs_ref[...])
    partial = jnp.zeros((16, 512), F32)
    for part in range(4):
        rows, columns = slice(256 * part, 256 * (part + 1)), slice(256 * part, 256 * (part + 1))
        factor_loads[part].wait()
        factor_high, factor_low = halves(u_ref[rows, :])
        u_high[c, rows, :] = factor_high
        u_low[c, rows, :] = factor_low
        high, low = rhs_high[:, columns], rhs_low[:, columns]
        both = dot_nn(jnp.concatenate([high, low], axis=0), factor_high)
        partial = partial + (both[:16] + both[16:] + dot_nn(high, factor_low))

    for load in loads[1:]:
        load.start()

    def load_columns(line, carry):
        for row in range(4):
            source = pl.multiple_of((line * 4 + row) * 128, 128)
            local(
                couple_hbm.at[:, pl.ds(source, 128)],
                couple_ref.at[c, row, :, pl.ds(pl.multiple_of(line * 128, 128), 128)],
                L_COUPLE,
            ).start()
        return carry

    lax.fori_loop(0, 8, load_columns, 0)

    part_ref[0] = partial[:8]
    part_ref[1] = partial[8:]
    pl.semaphore_wait(barrier, len(greeted))

    remote(part_ref.at[oc], sib_ref, PART, sibling).start()
    other_half = rhs_ref.at[pl.ds(pl.multiple_of(8 * oc, 8), 8), :]
    remote(other_half, both_ref.at[c], RHS, sibling).start()
    both_ref[c] = rhs_ref[pl.ds(pl.multiple_of(8 * c, 8), 8), :]
    arrived(sib_ref, PART)
    arrived(both_ref.at[oc], RHS)
    rhs = jnp.concatenate([both_ref[0], both_ref[1]], axis=1)

    def share_rest():
        for index in (L_DIAG, L_SELF, L_INTERP, L_SKEL):
            loads[index].wait()
        pick_ref[c] = jnp.zeros((2, 128, 512), BF16)
        put_ref[c] = jnp.zeros((2, 128, 512), BF16)
        square = lax.broadcasted_iota(jnp.int32, (32, 32), 0)
        square = (square == lax.broadcasted_iota(jnp.int32, (32, 32), 1)).astype(F32)
        turned = dot_nt(square.astype(BF16), skel_ref[...].astype(F32).astype(BF16))
        panel = lax.broadcasted_iota(jnp.int32, (32, 128), 1).astype(F32)
        for b in range(8):
            rows = slice(32 * (b % 4), 32 * (b % 4 + 1))
            columns = slice(128 * (b % 4), 128 * (b % 4 + 1))
            chosen = (panel == turned[:, b : b + 1]).astype(F32)
            pick_ref[c, b // 4, rows, columns] = chosen.astype(BF16)
            put_ref[c, b // 4, rows, columns] = interp_ref[b]
        for ref, phase in (
            (u_high, HIGH), (u_low, LOW), (diag_ref, DIAG), (self_ref, SELF), (pick_ref, PICK),
            (put_ref, PUT),
        ):
            remote(ref.at[c], ref.at[c], phase, sibling).start()

    def share_coupling():
        local(couple_ref.at[c], couple_ref.at[c], L_COUPLE).wait()
        remote(couple_ref.at[c], couple_ref.at[c], COUPLE, sibling).start()

    raw, total = all_reduce(
        0, part_ref[c] + sib_ref[...], share_rest, row_of([lane_sum(rhs * rhs)]), share_coupling
    )
    for ref, phase in (
        (u_high, HIGH), (u_low, LOW), (diag_ref, DIAG), (self_ref, SELF), (pick_ref, PICK),
        (put_ref, PUT),
    ):
        arrived(ref.at[oc], phase)
    beta_row = jnp.sqrt(total + EPS)
    beta = column_of(beta_row)
    first = rhs / beta
    first_coeffs = raw / beta
    diag = jnp.concatenate([diag_ref[0], diag_ref[1]], axis=1)
    z_ref[0] = diag * first - expand(first_coeffs)
    norm_one = lane_sum(first * first)
    safe_one = jnp.where(norm_one > 1e-12, norm_one, 1.0)

    def along(inner, norm, safe):
        return jnp.where(norm > 1e-12, inner / safe, 0.0)

    residue = operate(0)

    def first_stats():
        own = along(lane_sum(residue * first), norm_one, safe_one)
        rest = residue - own * first
        send_stats(
            1, PHASES + STAT, [own, lane_sum(rest * first), norm_one, lane_sum(rest * rest)]
        )

    raw, _ = all_reduce(1, project(residue), first_stats)
    stats = read_stats(1, PHASES + STAT)

    def fields_of(stats, count):
        return [stats] + [pltpu.roll(stats, 128 - 8 * i, 1) for i in range(1, count)]

    def rows_sum(value):
        return jnp.sum(value, axis=0, keepdims=True)

    own, cross, norm, rest = fields_of(stats, 4)
    h11_row = rows_sum(cross + own * norm)
    shift = own - h11_row
    square = rows_sum(rest + 2.0 * shift * cross + shift * shift * norm)
    h21_row = jnp.sqrt(jnp.maximum(square, 0.0) + EPS)
    h11 = column_of(h11_row)
    h21 = column_of(h21_row)
    second = (residue - h11 * first) / h21
    second_coeffs = (raw - h11 * first_coeffs) / h21
    z_ref[1] = diag * second - expand(second_coeffs)
    norm_two = lane_sum(second * second)
    mixed = lane_sum(first * second)
    safe_two = jnp.where(norm_two > 1e-12, norm_two, 1.0)

    residue = operate(1)
    own_one = along(lane_sum(residue * first), norm_one, safe_one)
    rest = residue - own_one * first
    own_two = along(lane_sum(rest * second), norm_two, safe_two)
    rest = rest - own_two * second
    send_stats(
        2,
        FINAL,
        [
            own_one, own_two, lane_sum(rest * first), lane_sum(rest * second),
            norm_one, mixed, norm_two, lane_sum(rest * rest),
        ],
    )
    stats = read_stats(2, FINAL)
    own_one, own_two, cross_one, cross_two, n11, n12, n22, rest = fields_of(stats, 8)
    h12_row = rows_sum(cross_one + own_one * n11 + own_two * n12)
    h22_row = rows_sum(cross_two + own_one * n12 + own_two * n22)
    shift_one = own_one - h12_row
    shift_two = own_two - h22_row
    square = rows_sum(
        rest
        + 2.0 * (shift_one * cross_one + shift_two * cross_two)
        + shift_one * shift_one * n11
        + 2.0 * shift_one * shift_two * n12
        + shift_two * shift_two * n22
    )
    h32_row = jnp.sqrt(jnp.maximum(square, 0.0) + EPS)
    radius_one = jnp.sqrt(h11_row * h11_row + h21_row * h21_row)
    cos_one = h11_row / radius_one
    sin_one = h21_row / radius_one
    upper = cos_one * h12_row + sin_one * h22_row
    lower = cos_one * h22_row - sin_one * h12_row
    radius_two = jnp.sqrt(lower * lower + h32_row * h32_row)
    step_two = lower / radius_two * (-sin_one * beta_row) / radius_two
    step_one = (cos_one * beta_row - upper * step_two) / radius_one
    result = column_of(step_one) * z_ref[0] + column_of(step_two) * z_ref[1]
    result_ref[0] = result[:, :1024]
    result_ref[1] = result[:, 1024:]
    remote(result_ref.at[oc], other_ref, RESULT, sibling).start()
    out_ref[pl.ds(pl.multiple_of(8 * c, 8), 8), :] = result_ref[c]
    arrived(other_ref, RESULT)
    out_ref[pl.ds(pl.multiple_of(8 * oc, 8), 8), :] = other_ref[...]

    sent(sib_ref, PART)
    sent(both_ref.at[c], RHS)
    for ref, phase in (
        (u_high, HIGH), (u_low, LOW), (diag_ref, DIAG), (self_ref, SELF), (pick_ref, PICK),
        (put_ref, PUT), (couple_ref, COUPLE),
    ):
        sent(ref.at[c], phase)
    sent(line_ref.at[pl.ds(1, 3)], ROW_Y)
    sent(line_ref.at[pl.ds(5, 7)], ROW_Z)
    sent(stat_ref.at[1, pl.ds(0, 31), :], PHASES + STAT)
    sent(stat_ref.at[2, pl.ds(0, 31), :], FINAL)
    sent(other_ref, RESULT)
    for m in range(2):
        base = m * PHASES
        sent(y_ref.at[m, pl.ds(1, 3)], base + YAX)
        sent(zax_ref.at[m, pl.ds(1, 7)], base + ZAX)
        sent(ext_ref.at[m, pl.ds(0, 16)], base + NEAR)
        sent(near_in.at[m, c], base + NEAR_BACK)
        sent(charge_in.at[m, pl.ds(0, 3)], base + CHARGE)
        for dz in EIGHT:
            sent(gather_ref.at[m, 0, :, pl.ds(0, 128)], base + LINE + dz)
        for dy in FOUR:
            sent(gather_ref.at[m, 0], base + PLANE + dy)
        sent(far_in.at[m, pl.ds(0, 3)], base + FAR)


def hbm(value):
    return pltpu.with_memory_space_constraint(value, pltpu.HBM)


def on_device(
    rhs_vec, self_coef, near_mats, near_ids, near_count, interp, skel_idx, coupling,
    diag_prec, low_rank,
):
    vmem = pltpu.VMEM
    return pl.pallas_call(
        kernel,
        out_shape=jax.ShapeDtypeStruct((16, 1024), F32),
        in_specs=[pl.BlockSpec(memory_space=pltpu.HBM)] * 10,
        out_specs=pl.BlockSpec(memory_space=pltpu.VMEM),
        scratch_shapes=[
            vmem((16, 1024), F32),
            vmem((2, 1, 1024), F32),
            vmem((8, 8, 128, 128), BF16),
            pltpu.SMEM((8, 8), jnp.int32),
            pltpu.SMEM((8,), jnp.int32),
            vmem((8, 32, 128), BF16),
            vmem((8, 32), jnp.int32),
            vmem((2, 4, 256, 1024), BF16),
            vmem((2, 1, 1024), F32),
            vmem((1024, 512), F32),
            vmem((2, 1024, 512), BF16),
            vmem((2, 1024, 512), BF16),
            vmem((2, 2, 128, 512), BF16),
            vmem((2, 2, 128, 512), BF16),
            vmem((2, 8, 2048), F32),
            vmem((8, 2048), F32),
            vmem((2, 8, 512), F32),
            vmem((8, 512), F32),
            vmem((2, 8, 1024), F32),
            vmem((2, 4, 8, 512), F32),
            vmem((2, 8, 8, 512), F32),
            vmem((12, 1, 128), F32),
            vmem((3, 1, 128), F32),
            vmem((3, 32, 128), F32),
            vmem((2, 16, 8, 128), F32),
            vmem((2, 24, 2, 8, 128), F32),
            vmem((2, 2, 8, 8, 128), F32),
            vmem((2, 2, 8, 8, 128), F32),
            vmem((2, 4, 8, 128), F32),
            vmem((2, 4, 8, 128), F32),
            vmem((2, 4, 32, 1024), BF16),
            vmem((2, 4, 2, 8, 256), F32),
            vmem((2, 4, 2, 8, 256), F32),
            vmem((2, 8, 1024), F32),
            vmem((8, 1024), F32),
            pltpu.SemaphoreType.DMA((RESULT + 1,)),
            pltpu.SemaphoreType.DMA((RESULT + 1,)),
            pltpu.SemaphoreType.DMA((L_U + 4,)),
        ],
        compiler_params=pltpu.CompilerParams(
            collective_id=0, has_side_effects=True, vmem_limit_bytes=24 * 1024 * 1024
        ),
        name="gmres",
    )(
        hbm(rhs_vec),
        hbm(self_coef.reshape(1, -1)),
        hbm(near_mats),
        hbm(near_ids),
        hbm(near_count),
        hbm(jnp.swapaxes(interp, 1, 2)),
        hbm(skel_idx),
        hbm(coupling.reshape(coupling.shape[0], coupling.shape[2])),
        hbm(diag_prec.reshape(1, -1)),
        hbm(low_rank),
    )


def solution(mesh):
    placed = (
        P("rhs", "space"),
        P("space"),
        P("space", None, None, None),
        P("space", None),
        P("space"),
        P("space", None, None),
        P("space", None),
        P("space", "rhs", None),
        P("space"),
        P("space", None),
    )
    return jax.shard_map(
        on_device, mesh=mesh, in_specs=placed, out_specs=P("rhs", "space"), check_vma=False
    )
```

```python
import jax
import jax.numpy as jnp
from jax import lax
from jax.experimental import pallas as pl
from jax.experimental.pallas import tpu as pltpu
from jax.sharding import PartitionSpec as P

EPS = 1e-06
F32 = jnp.float32
BF16 = jnp.bfloat16
MESH = pl.DeviceIdType.MESH

(YAX, ZAX, ROW_Y, ROW_Z, STAT, NEAR, NEAR_BACK, CHARGE, FAR, LINE) = range(10)
PLANE = LINE + 8
PHASES = PLANE + 4
(PART, RHS, DIAG, SELF, PICK, PUT, HIGH, LOW, COUPLE, FINAL) = range(2 * PHASES, 2 * PHASES + 10)
FOUR = (2, 1, 3)
EIGHT = (4, 3, 5, 2, 6, 1, 7)
PARTNERS = sorted(
    ((dz, dy) for dz in range(8) for dy in range(4)),
    key=lambda offset: -min(offset[0], 8 - offset[0]) - min(offset[1], 4 - offset[1]),
)
ORDER = (0, 1, 7, 2, 6, 3, 5, 4)
GROUPS = ((0,), (1, 7), (2, 6), (3, 5), (4,))
(L_RHS, L_DIAG, L_SELF, L_INTERP, L_SKEL, L_NEAR, L_IDS, L_COUNT, L_COUPLE, L_U) = range(10)


def dot_nn(a, b):
    return lax.dot_general(a, b, (((1,), (0,)), ((), ())), preferred_element_type=F32)


def dot_nt(a, b):
    return lax.dot_general(a, b, (((1,), (1,)), ((), ())), preferred_element_type=F32)


def halves(value):
    high = value.astype(BF16)
    return high, (value - high.astype(F32)).astype(BF16)


def stacked(pieces):
    return jnp.concatenate([piece.astype(F32) for piece in pieces], axis=0).astype(BF16)


def lane_sum(value):
    return jnp.sum(value, axis=1, keepdims=True)


def kernel(
    rhs_hbm, self_hbm, near_hbm, ids_hbm, count_hbm, interp_hbm, skel_hbm, couple_hbm,
    diag_hbm, u_hbm, out_ref,
    rhs_ref, self_ref, near_ref, ids_ref, count_ref, interp_ref, skel_ref, couple_ref, diag_ref,
    u_ref, u_high, u_low, pick_ref, put_ref, z_ref, w_ref,
    part_ref, sib_ref, both_ref, y_ref, zax_ref, line_ref, row_ref, stat_ref,
    blocks_ref, ext_ref, near_out, near_in, charge_out, charge_in, gather_ref, far_out, far_in,
    final_row, final_ref,
    send_sems, recv_sems, local_sems,
):
    s = lax.axis_index("space")
    x = lax.axis_index("rhs")
    z = s // 8
    y = (s // 2) % 4
    c = s % 2
    oc = 1 - c
    chip = s // 2
    sibling = (chip * 2 + oc, x)

    def local(src, dst, index):
        return pltpu.make_async_copy(src, dst, local_sems.at[index])

    def factor_rows(part):
        return pl.ds(256 * part, 256)

    factor_loads = [
        local(u_hbm.at[factor_rows(part)], u_ref.at[factor_rows(part)], L_U + part)
        for part in range(4)
    ]
    loads = [
        local(rhs_hbm, rhs_ref, L_RHS),
        local(diag_hbm, diag_ref.at[c], L_DIAG),
        local(self_hbm, self_ref.at[c], L_SELF),
        local(interp_hbm, interp_ref, L_INTERP),
        local(skel_hbm, skel_ref, L_SKEL),
        local(near_hbm, near_ref, L_NEAR),
        local(ids_hbm, ids_ref, L_IDS),
        local(count_hbm, count_ref, L_COUNT),
    ]
    loads[L_RHS].start()
    for load in factor_loads:
        load.start()

    lines = [lax.rem(z + dz, 8) for dz in range(8)]
    rows_on = [lax.rem(y + dy, 4) for dy in range(4)]
    groups = [lax.rem(x + dx, 4) for dx in range(4)]
    chips = [[line * 4 + row for row in rows_on] for line in lines]

    def at(dz=0, dy=0):
        return (chips[dz][dy] * 2 + c, x)

    def across(dx):
        return (s, groups[dx])

    barrier = pltpu.get_barrier_semaphore()
    greeted = [sibling] + [at(dz=dz) for dz in EIGHT] + [at(dy=dy) for dy in FOUR]
    greeted += [across(dx) for dx in FOUR]
    for device in greeted:
        pl.semaphore_signal(barrier, inc=1, device_id=device, device_id_type=MESH)

    def remote(src, dst, phase, device):
        return pltpu.make_async_remote_copy(
            src_ref=src,
            dst_ref=dst,
            send_sem=send_sems.at[phase],
            recv_sem=recv_sems.at[phase],
            device_id=device,
            device_id_type=MESH,
        )

    def arrived(ref, phase):
        remote(ref, ref, phase, sibling).wait_recv()

    def sent(ref, phase):
        remote(ref, ref, phase, sibling).wait_send()

    lane = lax.broadcasted_iota(jnp.int32, (8, 128), 1)
    excitation = lax.broadcasted_iota(jnp.int32, (8, 128), 0)

    def row_of(fields):
        total = jnp.zeros((8, 128), F32)
        for index, field in enumerate(fields):
            total = total + jnp.where(lane == index * 8 + excitation, field, 0.0)
        return jnp.sum(total, axis=0, keepdims=True)

    def column_of(row):
        return lane_sum(jnp.where(lane == excitation, row, 0.0))

    def project(value):
        high, low = halves(value)
        both = jnp.zeros((16, 512), F32)
        rest = jnp.zeros((8, 512), F32)
        stack = stacked([high, low])
        for region in range(2):
            columns = slice(1024 * region, 1024 * (region + 1))
            both = both + dot_nn(stack[:, columns], u_high[region])
            rest = rest + dot_nn(high[:, columns], u_low[region])
        return both[:8] + both[8:] + rest

    def expand(coeffs):
        high, low = halves(coeffs)
        stack = stacked([high, low])
        results = []
        for region in range(2):
            both = dot_nt(stack, u_high[region])
            results.append(both[:8] + both[8:] + dot_nt(high, u_low[region]))
        return jnp.concatenate(results, axis=1)

    def send_stats(index, phase, fields):
        row_ref[index] = row_of(fields)
        stat_ref[index, pl.ds(chip, 1), :] = row_ref[index]
        for dz, dy in PARTNERS[:-1]:
            remote(
                row_ref.at[index], stat_ref.at[index, pl.ds(chip, 1), :], phase, at(dz, dy)
            ).start()

    def read_stats(index, phase):
        arrived(stat_ref.at[index, pl.ds(0, 31), :], phase)
        return stat_ref[index]

    def all_reduce(m, partial, between, row=None, later=None):
        base = m * PHASES
        y_ref[m, 0] = partial
        for dy in FOUR:
            remote(y_ref.at[m, 0], y_ref.at[m, dy], base + YAX, at(dy=dy)).start()
        if row is not None:
            line_ref[0] = row
            for dy in FOUR:
                remote(line_ref.at[0], line_ref.at[dy], base + ROW_Y, at(dy=dy)).start()
        between()
        arrived(y_ref.at[m, pl.ds(1, 3)], base + YAX)
        zax_ref[m, 0] = (y_ref[m, 0] + y_ref[m, 1]) + (y_ref[m, 2] + y_ref[m, 3])
        for dz in EIGHT:
            remote(zax_ref.at[m, 0], zax_ref.at[m, dz], base + ZAX, at(dz=dz)).start()
        if row is not None:
            arrived(line_ref.at[pl.ds(1, 3)], base + ROW_Y)
            line_ref[4] = (line_ref[0] + line_ref[1]) + (line_ref[2] + line_ref[3])
            for dz in EIGHT:
                remote(line_ref.at[4], line_ref.at[4 + dz], base + ROW_Z, at(dz=dz)).start()
            later()
            arrived(line_ref.at[pl.ds(5, 7)], base + ROW_Z)
            pairs = [line_ref[4 + 2 * i] + line_ref[5 + 2 * i] for i in range(4)]
            row = (pairs[0] + pairs[1]) + (pairs[2] + pairs[3])
        arrived(zax_ref.at[m, pl.ds(1, 7)], base + ZAX)
        pairs = [zax_ref[m, 2 * i] + zax_ref[m, 2 * i + 1] for i in range(4)]
        return (pairs[0] + pairs[1]) + (pairs[2] + pairs[3]), row

    def operate(m):
        base = m * PHASES
        field = z_ref[m]
        low = field.astype(BF16)
        charges = []
        for region in range(2):
            for half in range(2):
                start = 1024 * region + 512 * half
                part = low[:, start : start + 512]
                charges.append(
                    dot_nt(part, pick_ref[region, half]) + dot_nt(part, put_ref[region, half])
                )
        for quarter in range(4):
            first_region, second_region = charges[quarter // 2], charges[2 + quarter // 2]
            if quarter % 2:
                first_region = pltpu.roll(first_region, 64, 1)
            else:
                second_region = pltpu.roll(second_region, 64, 1)
            charge_out[m, quarter] = jnp.where(lane < 64, first_region, second_region)
        for dx in FOUR:
            remote(
                charge_out.at[m, groups[dx]], charge_in.at[m, x], base + CHARGE, across(dx)
            ).start()
        charge_in[m, x] = charge_out[m, x]

        for i in range(16):
            block = field[:, 128 * i : 128 * (i + 1)]
            blocks_ref[m, i] = block
            ext_ref[m, 8 * oc + i, c] = block
        remote(
            blocks_ref.at[m], ext_ref.at[m, pl.ds(8 * c, 16), c], base + NEAR, sibling
        ).start()
        remote(
            blocks_ref.at[m, pl.ds(0, 8)],
            ext_ref.at[m, pl.ds(16, 8), c],
            base + NEAR,
            (((chip + 31) % 32) * 2 + 1, x),
        ).start()
        remote(
            blocks_ref.at[m, pl.ds(8, 8)],
            ext_ref.at[m, pl.ds(0, 8), c],
            base + NEAR,
            (((chip + 1) % 32) * 2, x),
        ).start()

        if m == 0:
            local(couple_ref.at[c], couple_ref.at[c], L_COUPLE).wait()
            remote(couple_ref.at[c], couple_ref.at[c], COUPLE, sibling).start()

        arrived(charge_in.at[m, pl.ds(0, 3)], base + CHARGE)
        block = jnp.concatenate([charge_in[m, i] for i in range(4)], axis=0).astype(BF16)

        def columns_of(offsets):
            first = ORDER.index(offsets[0])
            return gather_ref.at[m, y, :, pl.ds(128 * first, 128 * len(offsets))]

        columns_of((0,))[...] = block
        for dz in EIGHT:
            remote(columns_of((0,)), columns_of((dz,)), base + LINE + dz, at(dz=dz)).start()
        for group in GROUPS:
            for dz in group:
                if dz:
                    arrived(columns_of((dz,)), base + LINE + dz)
            for dy in FOUR:
                remote(
                    columns_of(group), columns_of(group), base + PLANE + dy, at(dy=dy)
                ).start()

        if m == 0:
            for index in (L_NEAR, L_IDS, L_COUNT):
                loads[index].wait()
        arrived(ext_ref.at[m, pl.ds(0, 16)], base + NEAR)
        for b in range(8):
            total = jnp.zeros((16, 128), F32)
            for pair in range(4):
                sides = []
                for k in (2 * pair, 2 * pair + 1):
                    source = jnp.clip(ids_ref[b, k] - (s - 1) * 8, 0, 23)
                    live = (k < count_ref[b]).astype(F32)
                    found = ext_ref[m, source].reshape(16, 128)
                    sides.append((found * live).astype(BF16))
                mats = jnp.concatenate([near_ref[b, 2 * pair], near_ref[b, 2 * pair + 1]], axis=1)
                total = total + dot_nt(jnp.concatenate(sides, axis=1), mats)
            near_out[m, 0, b] = total[:8]
            near_out[m, 1, b] = total[8:]
        remote(near_out.at[m, oc], near_in.at[m, c], base + NEAR_BACK, sibling).start()

        if m == 0:
            arrived(couple_ref.at[oc], COUPLE)

        def multiply(row):
            return [dot_nt(gather_ref[m, row], couple_ref[side, row]) for side in range(2)]

        parts = multiply(y)
        near_in[m, c] = near_out[m, c]
        arrived(near_in.at[m, oc], base + NEAR_BACK)
        for region in range(2):
            for b in range(8):
                start = 1024 * region + 128 * b
                columns = slice(start, start + 128)
                own_coef = self_ref[region, :, 128 * b : 128 * (b + 1)]
                w_ref[:, columns] = own_coef * field[:, columns] + near_in[m, region, b]
        for dy in FOUR[::-1]:
            arrived(gather_ref.at[m, rows_on[4 - dy]], base + PLANE + dy)
            parts = [a + b for a, b in zip(parts, multiply(rows_on[4 - dy]))]
        for i in range(4):
            for side in range(2):
                far_out[m, i, side] = parts[side][8 * i : 8 * (i + 1)]
        for dx in FOUR:
            remote(far_out.at[m, groups[dx]], far_in.at[m, x], base + FAR, across(dx)).start()
        far_in[m, x] = far_out[m, x]
        arrived(far_in.at[m, pl.ds(0, 3)], base + FAR)
        results = []
        for side in range(2):
            far = (far_in[m, 0, side] + far_in[m, 1, side]) + (
                far_in[m, 2, side] + far_in[m, 3, side]
            )
            for half in range(2):
                part = far[:, 128 * half : 128 * (half + 1)]
                high, _ = halves(part)
                rest_high, rest_low = halves(part - high.astype(F32))
                stack = stacked([high, rest_high, rest_low])
                spread_out = dot_nn(stack, pick_ref[side, half]) + dot_nn(stack, put_ref[side, half])
                results.append(spread_out[:8] + spread_out[8:16] + spread_out[16:])
        return w_ref[...] + jnp.concatenate(results, axis=1)

    loads[L_RHS].wait()
    rhs_high, rhs_low = halves(rhs_ref[...])
    partial = jnp.zeros((16, 512), F32)
    for part in range(4):
        rows, columns = slice(256 * part, 256 * (part + 1)), slice(256 * part, 256 * (part + 1))
        factor_loads[part].wait()
        factor_high, factor_low = halves(u_ref[rows, :])
        u_high[c, rows, :] = factor_high
        u_low[c, rows, :] = factor_low
        high, low = rhs_high[:, columns], rhs_low[:, columns]
        both = dot_nn(jnp.concatenate([high, low], axis=0), factor_high)
        partial = partial + (both[:16] + both[16:] + dot_nn(high, factor_low))

    part_ref[0] = partial[:8]
    part_ref[1] = partial[8:]
    pl.semaphore_wait(barrier, len(greeted))

    remote(part_ref.at[oc], sib_ref, PART, sibling).start()
    other_half = rhs_ref.at[pl.ds(pl.multiple_of(8 * oc, 8), 8), :]
    remote(other_half, both_ref.at[c], RHS, sibling).start()
    both_ref[c] = rhs_ref[pl.ds(pl.multiple_of(8 * c, 8), 8), :]

    for load in loads[1:]:
        load.start()

    arrived(sib_ref, PART)
    arrived(both_ref.at[oc], RHS)
    rhs = jnp.concatenate([both_ref[0], both_ref[1]], axis=1)

    def load_columns():
        for place, dz in enumerate(ORDER):
            for row in range(4):
                source = pl.multiple_of((lines[(8 - dz) % 8] * 4 + row) * 128, 128)
                local(
                    couple_hbm.at[:, pl.ds(source, 128)],
                    couple_ref.at[c, row, :, pl.ds(128 * place, 128)],
                    L_COUPLE,
                ).start()

    def share_rest():
        for index in (L_DIAG, L_SELF, L_INTERP, L_SKEL):
            loads[index].wait()
        pick_ref[c] = jnp.zeros((2, 128, 512), BF16)
        put_ref[c] = jnp.zeros((2, 128, 512), BF16)
        square = lax.broadcasted_iota(jnp.int32, (32, 32), 0)
        square = (square == lax.broadcasted_iota(jnp.int32, (32, 32), 1)).astype(F32)
        turned = dot_nt(square.astype(BF16), skel_ref[...].astype(F32).astype(BF16))
        panel = lax.broadcasted_iota(jnp.int32, (32, 128), 1).astype(F32)
        for b in range(8):
            rows = slice(32 * (b % 4), 32 * (b % 4 + 1))
            columns = slice(128 * (b % 4), 128 * (b % 4 + 1))
            chosen = (panel == turned[:, b : b + 1]).astype(F32)
            pick_ref[c, b // 4, rows, columns] = chosen.astype(BF16)
            put_ref[c, b // 4, rows, columns] = interp_ref[b]
        load_columns()

    def share_coupling():
        for ref, phase in (
            (u_high, HIGH), (u_low, LOW), (diag_ref, DIAG), (self_ref, SELF), (pick_ref, PICK),
            (put_ref, PUT),
        ):
            remote(ref.at[c], ref.at[c], phase, sibling).start()

    raw, total = all_reduce(
        0, part_ref[c] + sib_ref[...], share_rest, row_of([lane_sum(rhs * rhs)]), share_coupling
    )
    for ref, phase in (
        (u_high, HIGH), (u_low, LOW), (diag_ref, DIAG), (self_ref, SELF), (pick_ref, PICK),
        (put_ref, PUT),
    ):
        arrived(ref.at[oc], phase)
    beta_row = jnp.sqrt(total + EPS)
    beta = column_of(beta_row)
    first = rhs / beta
    first_coeffs = raw / beta
    diag = jnp.concatenate([diag_ref[0], diag_ref[1]], axis=1)
    z_ref[0] = diag * first - expand(first_coeffs)
    norm_one = lane_sum(first * first)
    safe_one = jnp.where(norm_one > 1e-12, norm_one, 1.0)

    def along(inner, norm, safe):
        return jnp.where(norm > 1e-12, inner / safe, 0.0)

    residue = operate(0)

    def first_stats():
        own = along(lane_sum(residue * first), norm_one, safe_one)
        rest = residue - own * first
        send_stats(
            1, PHASES + STAT, [own, lane_sum(rest * first), norm_one, lane_sum(rest * rest)]
        )

    raw, _ = all_reduce(1, project(residue), first_stats)
    stats = read_stats(1, PHASES + STAT)

    def fields_of(stats, count):
        return [stats] + [pltpu.roll(stats, 128 - 8 * i, 1) for i in range(1, count)]

    def rows_sum(value):
        return jnp.sum(value, axis=0, keepdims=True)

    own, cross, norm, rest = fields_of(stats, 4)
    h11_row = rows_sum(cross + own * norm)
    shift = own - h11_row
    square = rows_sum(rest + 2.0 * shift * cross + shift * shift * norm)
    h21_row = jnp.sqrt(jnp.maximum(square, 0.0) + EPS)
    h11 = column_of(h11_row)
    h21 = column_of(h21_row)
    second = (residue - h11 * first) / h21
    second_coeffs = (raw - h11 * first_coeffs) / h21
    z_ref[1] = diag * second - expand(second_coeffs)
    norm_two = lane_sum(second * second)
    mixed = lane_sum(first * second)
    safe_two = jnp.where(norm_two > 1e-12, norm_two, 1.0)

    residue = operate(1)
    own_one = along(lane_sum(residue * first), norm_one, safe_one)
    rest = residue - own_one * first
    own_two = along(lane_sum(rest * second), norm_two, safe_two)
    rest = rest - own_two * second
    final_row[...] = row_of(
        [
            own_one, own_two, lane_sum(rest * first), lane_sum(rest * second),
            norm_one, mixed, norm_two, lane_sum(rest * rest), beta, h11, h21,
        ]
    )
    own_row = pl.ds(c * 32 + chip, 1)
    final_ref[own_row, :] = final_row[...]

    for dz, dy in PARTNERS:
        for core in (oc, c):
            if core is oc or dz or dy:
                target = (chips[dz][dy] * 2 + core, x)
                remote(final_row, final_ref.at[own_row, :], FINAL, target).start()

    sent(sib_ref, PART)
    sent(both_ref.at[c], RHS)
    for ref, phase in (
        (u_high, HIGH), (u_low, LOW), (diag_ref, DIAG), (self_ref, SELF), (pick_ref, PICK),
        (put_ref, PUT), (couple_ref, COUPLE),
    ):
        sent(ref.at[c], phase)
    sent(line_ref.at[pl.ds(1, 3)], ROW_Y)
    sent(line_ref.at[pl.ds(5, 7)], ROW_Z)
    sent(stat_ref.at[1, pl.ds(0, 31), :], PHASES + STAT)
    for m in range(2):
        base = m * PHASES
        sent(y_ref.at[m, pl.ds(1, 3)], base + YAX)
        sent(zax_ref.at[m, pl.ds(1, 7)], base + ZAX)
        sent(ext_ref.at[m, pl.ds(0, 16)], base + NEAR)
        sent(near_in.at[m, c], base + NEAR_BACK)
        sent(charge_in.at[m, pl.ds(0, 3)], base + CHARGE)
        for dz in EIGHT:
            sent(gather_ref.at[m, 0, :, pl.ds(0, 128)], base + LINE + dz)
        for dy in FOUR:
            sent(gather_ref.at[m, 0], base + PLANE + dy)
        sent(far_in.at[m, pl.ds(0, 3)], base + FAR)
    arrived(final_ref.at[pl.ds(0, 63), :], FINAL)
    sent(final_ref.at[pl.ds(0, 63), :], FINAL)

    for half in range(2):
        (
            own_one, own_two, cross_one, cross_two, n11, n12, n22, rest, beta_row, h11_row, h21_row
        ) = fields_of(final_ref[32 * half : 32 * (half + 1), :], 11)
        beta_row, h11_row, h21_row = beta_row[:1], h11_row[:1], h21_row[:1]
        h12_row = rows_sum(cross_one + own_one * n11 + own_two * n12)
        h22_row = rows_sum(cross_two + own_one * n12 + own_two * n22)
        shift_one = own_one - h12_row
        shift_two = own_two - h22_row
        square = rows_sum(
            rest
            + 2.0 * (shift_one * cross_one + shift_two * cross_two)
            + shift_one * shift_one * n11
            + 2.0 * shift_one * shift_two * n12
            + shift_two * shift_two * n22
        )
        h32_row = jnp.sqrt(jnp.maximum(square, 0.0) + EPS)
        radius_one = jnp.sqrt(h11_row * h11_row + h21_row * h21_row)
        cos_one = h11_row / radius_one
        sin_one = h21_row / radius_one
        upper = cos_one * h12_row + sin_one * h22_row
        lower = cos_one * h22_row - sin_one * h12_row
        radius_two = jnp.sqrt(lower * lower + h32_row * h32_row)
        step_two = lower / radius_two * (-sin_one * beta_row) / radius_two
        step_one = (cos_one * beta_row - upper * step_two) / radius_one
        column_one, column_two = column_of(step_one), column_of(step_two)
        for b in range(8):
            out_ref[8 * half : 8 * (half + 1), 128 * b : 128 * (b + 1)] = (
                column_one * ext_ref[0, 8 + b, half] + column_two * ext_ref[1, 8 + b, half]
            )


def hbm(value):
    return pltpu.with_memory_space_constraint(value, pltpu.HBM)


def on_device(
    rhs_vec, self_coef, near_mats, near_ids, near_count, interp, skel_idx, coupling,
    diag_prec, low_rank,
):
    vmem = pltpu.VMEM
    return pl.pallas_call(
        kernel,
        out_shape=jax.ShapeDtypeStruct((16, 1024), F32),
        in_specs=[pl.BlockSpec(memory_space=pltpu.HBM)] * 10,
        out_specs=pl.BlockSpec(memory_space=pltpu.VMEM),
        scratch_shapes=[
            vmem((16, 1024), F32),
            vmem((2, 1, 1024), F32),
            vmem((8, 8, 128, 128), BF16),
            pltpu.SMEM((8, 8), jnp.int32),
            pltpu.SMEM((8,), jnp.int32),
            vmem((8, 32, 128), BF16),
            vmem((8, 32), jnp.int32),
            vmem((2, 4, 256, 1024), BF16),
            vmem((2, 1, 1024), F32),
            vmem((1024, 512), F32),
            vmem((2, 1024, 512), BF16),
            vmem((2, 1024, 512), BF16),
            vmem((2, 2, 128, 512), BF16),
            vmem((2, 2, 128, 512), BF16),
            vmem((2, 8, 2048), F32),
            vmem((8, 2048), F32),
            vmem((2, 8, 512), F32),
            vmem((8, 512), F32),
            vmem((2, 8, 1024), F32),
            vmem((2, 4, 8, 512), F32),
            vmem((2, 8, 8, 512), F32),
            vmem((12, 1, 128), F32),
            vmem((3, 1, 128), F32),
            vmem((3, 32, 128), F32),
            vmem((2, 16, 8, 128), F32),
            vmem((2, 24, 2, 8, 128), F32),
            vmem((2, 2, 8, 8, 128), F32),
            vmem((2, 2, 8, 8, 128), F32),
            vmem((2, 4, 8, 128), F32),
            vmem((2, 4, 8, 128), F32),
            vmem((2, 4, 32, 1024), BF16),
            vmem((2, 4, 2, 8, 256), F32),
            vmem((2, 4, 2, 8, 256), F32),
            vmem((1, 128), F32),
            vmem((64, 128), F32),
            pltpu.SemaphoreType.DMA((FINAL + 1,)),
            pltpu.SemaphoreType.DMA((FINAL + 1,)),
            pltpu.SemaphoreType.DMA((L_U + 4,)),
        ],
        compiler_params=pltpu.CompilerParams(
            collective_id=0, has_side_effects=True, vmem_limit_bytes=24 * 1024 * 1024
        ),
        name="gmres",
    )(
        hbm(rhs_vec),
        hbm(self_coef.reshape(1, -1)),
        hbm(near_mats),
        hbm(near_ids),
        hbm(near_count),
        hbm(jnp.swapaxes(interp, 1, 2)),
        hbm(skel_idx),
        hbm(coupling.reshape(coupling.shape[0], coupling.shape[2])),
        hbm(diag_prec.reshape(1, -1)),
        hbm(low_rank),
    )


def solution(mesh):
    placed = (
        P("rhs", "space"),
        P("space"),
        P("space", None, None, None),
        P("space", None),
        P("space"),
        P("space", None, None),
        P("space", None),
        P("space", "rhs", None),
        P("space"),
        P("space", None),
    )
    return jax.shard_map(
        on_device, mesh=mesh, in_specs=placed, out_specs=P("rhs", "space"), check_vma=False
    )
```

```python
import jax
import jax.numpy as jnp
from jax import lax
from jax.experimental import pallas as pl
from jax.experimental.pallas import tpu as pltpu
from jax.sharding import PartitionSpec as P

EPS = 1e-06
F32 = jnp.float32
BF16 = jnp.bfloat16
MESH = pl.DeviceIdType.MESH

(YAX, ZAX, ROW_Y, ROW_Z, STAT, NEAR, NEAR_BACK, CHARGE, FAR, LINE) = range(10)
PLANE = LINE + 8
PHASES = PLANE + 4
(PART, RHS, DIAG, SELF, PICK, PUT, HIGH, LOW, COUPLE, FINAL) = range(2 * PHASES, 2 * PHASES + 10)
FOUR = (2, 1, 3)
EIGHT = (4, 3, 5, 2, 6, 1, 7)
PARTNERS = sorted(
    ((dz, dy) for dz in range(8) for dy in range(4)),
    key=lambda offset: -min(offset[0], 8 - offset[0]) - min(offset[1], 4 - offset[1]),
)
ORDER = (0, 1, 7, 2, 6, 3, 5, 4)
GROUPS = ((0,), (1, 7), (2, 6), (3, 5), (4,))
(L_RHS, L_DIAG, L_SELF, L_INTERP, L_SKEL, L_NEAR, L_IDS, L_COUNT, L_COUPLE, L_U) = range(10)


def dot_nn(a, b):
    return lax.dot_general(a, b, (((1,), (0,)), ((), ())), preferred_element_type=F32)


def dot_nt(a, b):
    return lax.dot_general(a, b, (((1,), (1,)), ((), ())), preferred_element_type=F32)


def halves(value):
    high = value.astype(BF16)
    return high, (value - high.astype(F32)).astype(BF16)


def stacked(pieces):
    return jnp.concatenate([piece.astype(F32) for piece in pieces], axis=0).astype(BF16)


def lane_sum(value):
    return jnp.sum(value, axis=1, keepdims=True)


def kernel(
    rhs_hbm, self_hbm, near_hbm, ids_hbm, count_hbm, interp_hbm, skel_hbm, couple_hbm,
    diag_hbm, u_hbm, out_ref,
    rhs_ref, self_ref, near_ref, ids_ref, count_ref, interp_ref, skel_ref, couple_ref, diag_ref,
    u_ref, u_high, u_low, skel_high, skel_low, pick_ref, put_ref, z_ref, w_ref,
    part_ref, sib_ref, both_ref, y_ref, zax_ref, line_ref, row_ref, stat_ref,
    blocks_ref, ext_ref, near_out, near_in, charge_out, charge_in, gather_ref, far_out, far_in,
    final_row, final_ref,
    send_sems, recv_sems, local_sems, ready_sem,
):
    s = lax.axis_index("space")
    x = lax.axis_index("rhs")
    z = s // 8
    y = (s // 2) % 4
    c = s % 2
    oc = 1 - c
    chip = s // 2
    sibling = (chip * 2 + oc, x)

    def local(src, dst, index):
        return pltpu.make_async_copy(src, dst, local_sems.at[index])

    def factor_rows(part):
        return pl.ds(256 * part, 256)

    factor_loads = [
        local(u_hbm.at[factor_rows(part)], u_ref.at[factor_rows(part)], L_U + part)
        for part in range(4)
    ]
    loads = [
        local(rhs_hbm, rhs_ref, L_RHS),
        local(diag_hbm, diag_ref.at[c], L_DIAG),
        local(self_hbm, self_ref.at[c], L_SELF),
        local(interp_hbm, interp_ref, L_INTERP),
        local(skel_hbm, skel_ref, L_SKEL),
        local(near_hbm, near_ref, L_NEAR),
        local(ids_hbm, ids_ref, L_IDS),
        local(count_hbm, count_ref, L_COUNT),
    ]
    loads[L_RHS].start()
    for load in factor_loads:
        load.start()

    lines = [lax.rem(z + dz, 8) for dz in range(8)]
    rows_on = [lax.rem(y + dy, 4) for dy in range(4)]
    groups = [lax.rem(x + dx, 4) for dx in range(4)]
    chips = [[line * 4 + row for row in rows_on] for line in lines]

    def at(dz=0, dy=0):
        return (chips[dz][dy] * 2 + c, x)

    def across(dx):
        return (s, groups[dx])

    barrier = pltpu.get_barrier_semaphore()
    greeted = [sibling] + [at(dz=dz) for dz in (2, 6, 1, 7)] + [at(dy=dy) for dy in FOUR]
    greeted += [across(dx) for dx in FOUR]
    for device in greeted:
        pl.semaphore_signal(barrier, inc=1, device_id=device, device_id_type=MESH)

    def remote(src, dst, phase, device):
        return pltpu.make_async_remote_copy(
            src_ref=src,
            dst_ref=dst,
            send_sem=send_sems.at[phase],
            recv_sem=recv_sems.at[phase],
            device_id=device,
            device_id_type=MESH,
        )

    def arrived(ref, phase):
        remote(ref, ref, phase, sibling).wait_recv()

    def sent(ref, phase):
        remote(ref, ref, phase, sibling).wait_send()

    lane = lax.broadcasted_iota(jnp.int32, (8, 128), 1)
    excitation = lax.broadcasted_iota(jnp.int32, (8, 128), 0)

    def row_of(fields):
        total = jnp.zeros((8, 128), F32)
        for index, field in enumerate(fields):
            total = total + jnp.where(lane == index * 8 + excitation, field, 0.0)
        return jnp.sum(total, axis=0, keepdims=True)

    def column_of(row):
        return lane_sum(jnp.where(lane == excitation, row, 0.0))

    def project(value):
        high, low = halves(value)
        both = jnp.zeros((16, 512), F32)
        rest = jnp.zeros((8, 512), F32)
        stack = stacked([high, low])
        for region in range(2):
            columns = slice(1024 * region, 1024 * (region + 1))
            both = both + dot_nn(stack[:, columns], u_high[region])
            rest = rest + dot_nn(high[:, columns], u_low[region])
        return both[:8] + both[8:] + rest

    def expand(coeffs):
        high, low = halves(coeffs)
        stack = stacked([high, low])
        results = []
        for region in range(2):
            both = dot_nt(stack, u_high[region])
            results.append(both[:8] + both[8:] + dot_nt(high, u_low[region]))
        return jnp.concatenate(results, axis=1)

    def send_stats(index, phase, fields):
        row_ref[index] = row_of(fields)
        stat_ref[index, pl.ds(chip, 1), :] = row_ref[index]
        for dz, dy in PARTNERS[:-1]:
            remote(
                row_ref.at[index], stat_ref.at[index, pl.ds(chip, 1), :], phase, at(dz, dy)
            ).start()

    def read_stats(index, phase):
        arrived(stat_ref.at[index, pl.ds(0, 31), :], phase)
        return stat_ref[index]

    def all_reduce(m, partial, between, row=None, later=None):
        base = m * PHASES
        y_ref[m, 0] = partial
        for dy in FOUR:
            remote(y_ref.at[m, 0], y_ref.at[m, dy], base + YAX, at(dy=dy)).start()
        if row is not None:
            line_ref[0] = row
            for dy in FOUR:
                remote(line_ref.at[0], line_ref.at[dy], base + ROW_Y, at(dy=dy)).start()
        between()
        arrived(y_ref.at[m, pl.ds(1, 3)], base + YAX)
        zax_ref[m, 0] = (y_ref[m, 0] + y_ref[m, 1]) + (y_ref[m, 2] + y_ref[m, 3])
        if m == 0:
            pl.semaphore_wait(ready_sem, 2)
        for dz in EIGHT:
            remote(zax_ref.at[m, 0], zax_ref.at[m, dz], base + ZAX, at(dz=dz)).start()
        if row is not None:
            arrived(line_ref.at[pl.ds(1, 3)], base + ROW_Y)
            line_ref[4] = (line_ref[0] + line_ref[1]) + (line_ref[2] + line_ref[3])
            for dz in EIGHT:
                remote(line_ref.at[4], line_ref.at[4 + dz], base + ROW_Z, at(dz=dz)).start()
            later()
            arrived(line_ref.at[pl.ds(5, 7)], base + ROW_Z)
            pairs = [line_ref[4 + 2 * i] + line_ref[5 + 2 * i] for i in range(4)]
            row = (pairs[0] + pairs[1]) + (pairs[2] + pairs[3])
        arrived(zax_ref.at[m, pl.ds(1, 7)], base + ZAX)
        pairs = [zax_ref[m, 2 * i] + zax_ref[m, 2 * i + 1] for i in range(4)]
        return (pairs[0] + pairs[1]) + (pairs[2] + pairs[3]), row

    def operate(m):
        base = m * PHASES
        field = z_ref[m]
        low = field.astype(BF16)
        charges = []
        for region in range(2):
            for half in range(2):
                start = 1024 * region + 512 * half
                part = low[:, start : start + 512]
                charges.append(
                    dot_nt(part, pick_ref[region, half]) + dot_nt(part, put_ref[region, half])
                )
        for quarter in range(4):
            first_region, second_region = charges[quarter // 2], charges[2 + quarter // 2]
            if quarter % 2:
                first_region = pltpu.roll(first_region, 64, 1)
            else:
                second_region = pltpu.roll(second_region, 64, 1)
            charge_out[m, quarter] = jnp.where(lane < 64, first_region, second_region)
        for dx in FOUR:
            remote(
                charge_out.at[m, groups[dx]], charge_in.at[m, x], base + CHARGE, across(dx)
            ).start()
        charge_in[m, x] = charge_out[m, x]

        for i in range(16):
            block = field[:, 128 * i : 128 * (i + 1)]
            blocks_ref[m, i] = block
            ext_ref[m, 8 * oc + i, c] = block
        remote(
            blocks_ref.at[m], ext_ref.at[m, pl.ds(8 * c, 16), c], base + NEAR, sibling
        ).start()
        remote(
            blocks_ref.at[m, pl.ds(0, 8)],
            ext_ref.at[m, pl.ds(16, 8), c],
            base + NEAR,
            (((chip + 31) % 32) * 2 + 1, x),
        ).start()
        remote(
            blocks_ref.at[m, pl.ds(8, 8)],
            ext_ref.at[m, pl.ds(0, 8), c],
            base + NEAR,
            (((chip + 1) % 32) * 2, x),
        ).start()

        if m == 0:
            local(couple_ref.at[c], couple_ref.at[c], L_COUPLE).wait()
            remote(couple_ref.at[c], couple_ref.at[c], COUPLE, sibling).start()

        if m == 0:
            for region in range(2):
                for half in range(2):
                    panels = slice(512 * half, 512 * (half + 1))
                    skeletons = slice(128 * half, 128 * (half + 1))
                    total = jnp.zeros((128, 512), F32)
                    for restriction in (pick_ref, put_ref):
                        for factor in (u_high, u_low):
                            total = total + dot_nn(
                                restriction[region, half], factor[region, panels, :]
                            )
                    high, low_part = halves(total)
                    skel_high[region, skeletons, :] = high
                    skel_low[region, skeletons, :] = low_part

        arrived(charge_in.at[m, pl.ds(0, 3)], base + CHARGE)
        block = jnp.concatenate([charge_in[m, i] for i in range(4)], axis=0).astype(BF16)

        def columns_of(offsets):
            first = ORDER.index(offsets[0])
            return gather_ref.at[m, y, :, pl.ds(128 * first, 128 * len(offsets))]

        columns_of((0,))[...] = block
        for dz in EIGHT:
            remote(columns_of((0,)), columns_of((dz,)), base + LINE + dz, at(dz=dz)).start()
        for group in GROUPS:
            for dz in group:
                if dz:
                    arrived(columns_of((dz,)), base + LINE + dz)
            for dy in FOUR:
                remote(
                    columns_of(group), columns_of(group), base + PLANE + dy, at(dy=dy)
                ).start()

        if m == 0:
            for index in (L_NEAR, L_IDS, L_COUNT):
                loads[index].wait()
        arrived(ext_ref.at[m, pl.ds(0, 16)], base + NEAR)
        for b in range(8):
            total = jnp.zeros((16, 128), F32)
            for pair in range(4):
                sides = []
                for k in (2 * pair, 2 * pair + 1):
                    source = jnp.clip(ids_ref[b, k] - (s - 1) * 8, 0, 23)
                    live = (k < count_ref[b]).astype(F32)
                    found = ext_ref[m, source].reshape(16, 128)
                    sides.append((found * live).astype(BF16))
                mats = jnp.concatenate([near_ref[b, 2 * pair], near_ref[b, 2 * pair + 1]], axis=1)
                total = total + dot_nt(jnp.concatenate(sides, axis=1), mats)
            near_out[m, 0, b] = total[:8]
            near_out[m, 1, b] = total[8:]
        remote(near_out.at[m, oc], near_in.at[m, c], base + NEAR_BACK, sibling).start()

        if m == 0:
            arrived(couple_ref.at[oc], COUPLE)

        def multiply(row):
            return [dot_nt(gather_ref[m, row], couple_ref[side, row]) for side in range(2)]

        parts = multiply(y)
        near_in[m, c] = near_out[m, c]
        arrived(near_in.at[m, oc], base + NEAR_BACK)
        for region in range(2):
            for b in range(8):
                start = 1024 * region + 128 * b
                columns = slice(start, start + 128)
                own_coef = self_ref[region, :, 128 * b : 128 * (b + 1)]
                w_ref[:, columns] = own_coef * field[:, columns] + near_in[m, region, b]
        for dy in FOUR[::-1]:
            arrived(gather_ref.at[m, rows_on[4 - dy]], base + PLANE + dy)
            parts = [a + b for a, b in zip(parts, multiply(rows_on[4 - dy]))]
        for i in range(4):
            for side in range(2):
                far_out[m, i, side] = parts[side][8 * i : 8 * (i + 1)]
        for dx in FOUR:
            remote(far_out.at[m, groups[dx]], far_in.at[m, x], base + FAR, across(dx)).start()
        far_in[m, x] = far_out[m, x]
        projected = project(w_ref[...]) if m == 0 else None
        arrived(far_in.at[m, pl.ds(0, 3)], base + FAR)
        fars = [
            (far_in[m, 0, side] + far_in[m, 1, side]) + (far_in[m, 2, side] + far_in[m, 3, side])
            for side in range(2)
        ]
        if m == 0:
            for side in range(2):
                high, rest = halves(fars[side])
                both = dot_nn(stacked([high, rest]), skel_high[side])
                projected = projected + (both[:8] + both[8:] + dot_nn(high, skel_low[side]))

        def finish():
            results = []
            for side in range(2):
                for half in range(2):
                    part = fars[side][:, 128 * half : 128 * (half + 1)]
                    high, _ = halves(part)
                    rest_high, rest_low = halves(part - high.astype(F32))
                    stack = stacked([high, rest_high, rest_low])
                    spread_out = dot_nn(stack, pick_ref[side, half]) + dot_nn(
                        stack, put_ref[side, half]
                    )
                    results.append(spread_out[:8] + spread_out[8:16] + spread_out[16:])
            return w_ref[...] + jnp.concatenate(results, axis=1)

        return finish, projected

    loads[L_RHS].wait()
    rhs_high, rhs_low = halves(rhs_ref[...])
    partial = jnp.zeros((16, 512), F32)
    for part in range(4):
        rows, columns = slice(256 * part, 256 * (part + 1)), slice(256 * part, 256 * (part + 1))
        factor_loads[part].wait()
        factor_high, factor_low = halves(u_ref[rows, :])
        u_high[c, rows, :] = factor_high
        u_low[c, rows, :] = factor_low
        high, low = rhs_high[:, columns], rhs_low[:, columns]
        both = dot_nn(jnp.concatenate([high, low], axis=0), factor_high)
        partial = partial + (both[:16] + both[16:] + dot_nn(high, factor_low))

    part_ref[0] = partial[:8]
    part_ref[1] = partial[8:]
    pl.semaphore_wait(barrier, len(greeted))

    remote(part_ref.at[oc], sib_ref, PART, sibling).start()
    other_half = rhs_ref.at[pl.ds(pl.multiple_of(8 * oc, 8), 8), :]
    remote(other_half, both_ref.at[c], RHS, sibling).start()
    for dz in (2, 6):
        pl.semaphore_signal(ready_sem, inc=1, device_id=at(dz=dz), device_id_type=MESH)
    both_ref[c] = rhs_ref[pl.ds(pl.multiple_of(8 * c, 8), 8), :]

    for load in loads[1:]:
        load.start()

    arrived(sib_ref, PART)
    arrived(both_ref.at[oc], RHS)
    rhs = jnp.concatenate([both_ref[0], both_ref[1]], axis=1)

    def load_columns():
        for place, dz in enumerate(ORDER):
            for row in range(4):
                source = pl.multiple_of((lines[(8 - dz) % 8] * 4 + row) * 128, 128)
                local(
                    couple_hbm.at[:, pl.ds(source, 128)],
                    couple_ref.at[c, row, :, pl.ds(128 * place, 128)],
                    L_COUPLE,
                ).start()

    def share_rest():
        for index in (L_DIAG, L_SELF, L_INTERP, L_SKEL):
            loads[index].wait()
        pick_ref[c] = jnp.zeros((2, 128, 512), BF16)
        put_ref[c] = jnp.zeros((2, 128, 512), BF16)
        square = lax.broadcasted_iota(jnp.int32, (32, 32), 0)
        square = (square == lax.broadcasted_iota(jnp.int32, (32, 32), 1)).astype(F32)
        turned = dot_nt(square.astype(BF16), skel_ref[...].astype(F32).astype(BF16))
        panel = lax.broadcasted_iota(jnp.int32, (32, 128), 1).astype(F32)
        for b in range(8):
            rows = slice(32 * (b % 4), 32 * (b % 4 + 1))
            columns = slice(128 * (b % 4), 128 * (b % 4 + 1))
            chosen = (panel == turned[:, b : b + 1]).astype(F32)
            pick_ref[c, b // 4, rows, columns] = chosen.astype(BF16)
            put_ref[c, b // 4, rows, columns] = interp_ref[b]
        load_columns()

    def share_coupling():
        for ref, phase in (
            (u_high, HIGH), (u_low, LOW), (diag_ref, DIAG), (self_ref, SELF), (pick_ref, PICK),
            (put_ref, PUT),
        ):
            remote(ref.at[c], ref.at[c], phase, sibling).start()

    raw, total = all_reduce(
        0, part_ref[c] + sib_ref[...], share_rest, row_of([lane_sum(rhs * rhs)]), share_coupling
    )
    for ref, phase in (
        (u_high, HIGH), (u_low, LOW), (diag_ref, DIAG), (self_ref, SELF), (pick_ref, PICK),
        (put_ref, PUT),
    ):
        arrived(ref.at[oc], phase)
    beta_row = jnp.sqrt(total + EPS)
    beta = column_of(beta_row)
    first = rhs / beta
    first_coeffs = raw / beta
    diag = jnp.concatenate([diag_ref[0], diag_ref[1]], axis=1)
    z_ref[0] = diag * first - expand(first_coeffs)
    norm_one = lane_sum(first * first)
    safe_one = jnp.where(norm_one > 1e-12, norm_one, 1.0)

    def along(inner, norm, safe):
        return jnp.where(norm > 1e-12, inner / safe, 0.0)

    finish, projected = operate(0)
    residues = []

    def first_stats():
        residue = finish()
        residues.append(residue)
        own = along(lane_sum(residue * first), norm_one, safe_one)
        rest = residue - own * first
        send_stats(
            1, PHASES + STAT, [own, lane_sum(rest * first), norm_one, lane_sum(rest * rest)]
        )

    raw, _ = all_reduce(1, projected, first_stats)
    residue = residues[0]
    stats = read_stats(1, PHASES + STAT)

    def fields_of(stats, count):
        return [stats] + [pltpu.roll(stats, 128 - 8 * i, 1) for i in range(1, count)]

    def rows_sum(value):
        return jnp.sum(value, axis=0, keepdims=True)

    own, cross, norm, rest = fields_of(stats, 4)
    h11_row = rows_sum(cross + own * norm)
    shift = own - h11_row
    square = rows_sum(rest + 2.0 * shift * cross + shift * shift * norm)
    h21_row = jnp.sqrt(jnp.maximum(square, 0.0) + EPS)
    h11 = column_of(h11_row)
    h21 = column_of(h21_row)
    second = (residue - h11 * first) / h21
    second_coeffs = (raw - h11 * first_coeffs) / h21
    z_ref[1] = diag * second - expand(second_coeffs)
    norm_two = lane_sum(second * second)
    mixed = lane_sum(first * second)
    safe_two = jnp.where(norm_two > 1e-12, norm_two, 1.0)

    residue = operate(1)[0]()
    own_one = along(lane_sum(residue * first), norm_one, safe_one)
    rest = residue - own_one * first
    own_two = along(lane_sum(rest * second), norm_two, safe_two)
    rest = rest - own_two * second
    final_row[...] = row_of(
        [
            own_one, own_two, lane_sum(rest * first), lane_sum(rest * second),
            norm_one, mixed, norm_two, lane_sum(rest * rest), beta, h11, h21,
        ]
    )
    own_row = pl.ds(c * 32 + chip, 1)
    final_ref[own_row, :] = final_row[...]

    for dz, dy in PARTNERS:
        for core in (oc, c):
            if core is oc or dz or dy:
                target = (chips[dz][dy] * 2 + core, x)
                remote(final_row, final_ref.at[own_row, :], FINAL, target).start()

    sent(sib_ref, PART)
    sent(both_ref.at[c], RHS)
    for ref, phase in (
        (u_high, HIGH), (u_low, LOW), (diag_ref, DIAG), (self_ref, SELF), (pick_ref, PICK),
        (put_ref, PUT), (couple_ref, COUPLE),
    ):
        sent(ref.at[c], phase)
    sent(line_ref.at[pl.ds(1, 3)], ROW_Y)
    sent(line_ref.at[pl.ds(5, 7)], ROW_Z)
    sent(stat_ref.at[1, pl.ds(0, 31), :], PHASES + STAT)
    for m in range(2):
        base = m * PHASES
        sent(y_ref.at[m, pl.ds(1, 3)], base + YAX)
        sent(zax_ref.at[m, pl.ds(1, 7)], base + ZAX)
        sent(ext_ref.at[m, pl.ds(0, 16)], base + NEAR)
        sent(near_in.at[m, c], base + NEAR_BACK)
        sent(charge_in.at[m, pl.ds(0, 3)], base + CHARGE)
        for dz in EIGHT:
            sent(gather_ref.at[m, 0, :, pl.ds(0, 128)], base + LINE + dz)
        for dy in FOUR:
            sent(gather_ref.at[m, 0], base + PLANE + dy)
        sent(far_in.at[m, pl.ds(0, 3)], base + FAR)
    arrived(final_ref.at[pl.ds(0, 63), :], FINAL)
    sent(final_ref.at[pl.ds(0, 63), :], FINAL)

    for half in range(2):
        (
            own_one, own_two, cross_one, cross_two, n11, n12, n22, rest, beta_row, h11_row, h21_row
        ) = fields_of(final_ref[32 * half : 32 * (half + 1), :], 11)
        beta_row, h11_row, h21_row = beta_row[:1], h11_row[:1], h21_row[:1]
        h12_row = rows_sum(cross_one + own_one * n11 + own_two * n12)
        h22_row = rows_sum(cross_two + own_one * n12 + own_two * n22)
        shift_one = own_one - h12_row
        shift_two = own_two - h22_row
        square = rows_sum(
            rest
            + 2.0 * (shift_one * cross_one + shift_two * cross_two)
            + shift_one * shift_one * n11
            + 2.0 * shift_one * shift_two * n12
            + shift_two * shift_two * n22
        )
        h32_row = jnp.sqrt(jnp.maximum(square, 0.0) + EPS)
        radius_one = jnp.sqrt(h11_row * h11_row + h21_row * h21_row)
        cos_one = h11_row / radius_one
        sin_one = h21_row / radius_one
        upper = cos_one * h12_row + sin_one * h22_row
        lower = cos_one * h22_row - sin_one * h12_row
        radius_two = jnp.sqrt(lower * lower + h32_row * h32_row)
        step_two = lower / radius_two * (-sin_one * beta_row) / radius_two
        step_one = (cos_one * beta_row - upper * step_two) / radius_one
        column_one, column_two = column_of(step_one), column_of(step_two)
        for b in range(8):
            out_ref[8 * half : 8 * (half + 1), 128 * b : 128 * (b + 1)] = (
                column_one * ext_ref[0, 8 + b, half] + column_two * ext_ref[1, 8 + b, half]
            )


def hbm(value):
    return pltpu.with_memory_space_constraint(value, pltpu.HBM)


def on_device(
    rhs_vec, self_coef, near_mats, near_ids, near_count, interp, skel_idx, coupling,
    diag_prec, low_rank,
):
    vmem = pltpu.VMEM
    return pl.pallas_call(
        kernel,
        out_shape=jax.ShapeDtypeStruct((16, 1024), F32),
        in_specs=[pl.BlockSpec(memory_space=pltpu.HBM)] * 10,
        out_specs=pl.BlockSpec(memory_space=pltpu.VMEM),
        scratch_shapes=[
            vmem((16, 1024), F32),
            vmem((2, 1, 1024), F32),
            vmem((8, 8, 128, 128), BF16),
            pltpu.SMEM((8, 8), jnp.int32),
            pltpu.SMEM((8,), jnp.int32),
            vmem((8, 32, 128), BF16),
            vmem((8, 32), jnp.int32),
            vmem((2, 4, 256, 1024), BF16),
            vmem((2, 1, 1024), F32),
            vmem((1024, 512), F32),
            vmem((2, 1024, 512), BF16),
            vmem((2, 1024, 512), BF16),
            vmem((2, 256, 512), BF16),
            vmem((2, 256, 512), BF16),
            vmem((2, 2, 128, 512), BF16),
            vmem((2, 2, 128, 512), BF16),
            vmem((2, 8, 2048), F32),
            vmem((8, 2048), F32),
            vmem((2, 8, 512), F32),
            vmem((8, 512), F32),
            vmem((2, 8, 1024), F32),
            vmem((2, 4, 8, 512), F32),
            vmem((2, 8, 8, 512), F32),
            vmem((12, 1, 128), F32),
            vmem((3, 1, 128), F32),
            vmem((3, 32, 128), F32),
            vmem((2, 16, 8, 128), F32),
            vmem((2, 24, 2, 8, 128), F32),
            vmem((2, 2, 8, 8, 128), F32),
            vmem((2, 2, 8, 8, 128), F32),
            vmem((2, 4, 8, 128), F32),
            vmem((2, 4, 8, 128), F32),
            vmem((2, 4, 32, 1024), BF16),
            vmem((2, 4, 2, 8, 256), F32),
            vmem((2, 4, 2, 8, 256), F32),
            vmem((1, 128), F32),
            vmem((64, 128), F32),
            pltpu.SemaphoreType.DMA((FINAL + 1,)),
            pltpu.SemaphoreType.DMA((FINAL + 1,)),
            pltpu.SemaphoreType.DMA((L_U + 4,)),
            pltpu.SemaphoreType.REGULAR,
        ],
        compiler_params=pltpu.CompilerParams(
            collective_id=0, has_side_effects=True, vmem_limit_bytes=24 * 1024 * 1024
        ),
        name="gmres",
    )(
        hbm(rhs_vec),
        hbm(self_coef.reshape(1, -1)),
        hbm(near_mats),
        hbm(near_ids),
        hbm(near_count),
        hbm(jnp.swapaxes(interp, 1, 2)),
        hbm(skel_idx),
        hbm(coupling.reshape(coupling.shape[0], coupling.shape[2])),
        hbm(diag_prec.reshape(1, -1)),
        hbm(low_rank),
    )


def solution(mesh):
    placed = (
        P("rhs", "space"),
        P("space"),
        P("space", None, None, None),
        P("space", None),
        P("space"),
        P("space", None, None),
        P("space", None),
        P("space", "rhs", None),
        P("space"),
        P("space", None),
    )
    return jax.shard_map(
        on_device, mesh=mesh, in_specs=placed, out_specs=P("rhs", "space"), check_vma=False
    )
```

```python
import jax
import jax.numpy as jnp
from jax import lax
from jax.experimental import pallas as pl
from jax.experimental.pallas import tpu as pltpu
from jax.sharding import PartitionSpec as P

EPS = 1e-06
F32 = jnp.float32
BF16 = jnp.bfloat16
MESH = pl.DeviceIdType.MESH

(YAX, ZAX, ROW_Y, ROW_Z, STAT, NEAR, NEAR_BACK, CHARGE, FAR, LINE) = range(10)
PLANE = LINE + 8
PHASES = PLANE + 4
(PART, RHS, DIAG, SELF, PICK, PUT, HIGH, LOW, COUPLE, FINAL) = range(2 * PHASES, 2 * PHASES + 10)
FOUR = (2, 1, 3)
EIGHT = (4, 3, 5, 2, 6, 1, 7)
PARTNERS = sorted(
    ((dz, dy) for dz in range(8) for dy in range(4)),
    key=lambda offset: -min(offset[0], 8 - offset[0]) - min(offset[1], 4 - offset[1]),
)
ORDER = (0, 1, 7, 2, 6, 3, 5, 4)
GROUPS = ((0,), (1, 7), (2, 6), (3, 5), (4,))
(L_RHS, L_DIAG, L_SELF, L_INTERP, L_SKEL, L_NEAR, L_IDS, L_COUNT, L_COUPLE, L_U) = range(10)


def dot_nn(a, b):
    return lax.dot_general(a, b, (((1,), (0,)), ((), ())), preferred_element_type=F32)


def dot_nt(a, b):
    return lax.dot_general(a, b, (((1,), (1,)), ((), ())), preferred_element_type=F32)


def halves(value):
    high = value.astype(BF16)
    return high, (value - high.astype(F32)).astype(BF16)


def stacked(pieces):
    return jnp.concatenate([piece.astype(F32) for piece in pieces], axis=0).astype(BF16)


def lane_sum(value):
    return jnp.sum(value, axis=1, keepdims=True)


def kernel(
    rhs_hbm, self_hbm, near_hbm, ids_hbm, count_hbm, interp_hbm, skel_hbm, couple_hbm,
    diag_hbm, u_hbm, out_ref,
    rhs_ref, self_ref, near_ref, ids_ref, count_ref, interp_ref, skel_ref, couple_ref, diag_ref,
    u_ref, u_high, u_low, skel_high, skel_low, pick_ref, put_ref, z_ref, w_ref,
    part_ref, sib_ref, both_ref, y_ref, zax_ref, line_ref, row_ref, stat_ref,
    blocks_ref, ext_ref, near_out, near_in, charge_out, charge_in, gather_ref, far_out, far_in,
    final_row, final_ref,
    send_sems, recv_sems, local_sems, ready_sem,
):
    s = lax.axis_index("space")
    x = lax.axis_index("rhs")
    z = s // 8
    y = (s // 2) % 4
    c = s % 2
    oc = 1 - c
    chip = s // 2
    sibling = (chip * 2 + oc, x)

    def local(src, dst, index):
        return pltpu.make_async_copy(src, dst, local_sems.at[index])

    def factor_rows(part):
        return pl.ds(256 * part, 256)

    factor_loads = [
        local(u_hbm.at[factor_rows(part)], u_ref.at[factor_rows(part)], L_U + part)
        for part in range(4)
    ]
    loads = [
        local(rhs_hbm, rhs_ref, L_RHS),
        local(diag_hbm, diag_ref.at[c], L_DIAG),
        local(self_hbm, self_ref.at[c], L_SELF),
        local(interp_hbm, interp_ref, L_INTERP),
        local(skel_hbm, skel_ref, L_SKEL),
        local(near_hbm, near_ref, L_NEAR),
        local(ids_hbm, ids_ref, L_IDS),
        local(count_hbm, count_ref, L_COUNT),
    ]
    loads[L_RHS].start()
    for load in factor_loads:
        load.start()

    lines = [lax.rem(z + dz, 8) for dz in range(8)]
    rows_on = [lax.rem(y + dy, 4) for dy in range(4)]
    groups = [lax.rem(x + dx, 4) for dx in range(4)]
    chips = [[line * 4 + row for row in rows_on] for line in lines]

    def at(dz=0, dy=0):
        return (chips[dz][dy] * 2 + c, x)

    def across(dx):
        return (s, groups[dx])

    barrier = pltpu.get_barrier_semaphore()
    greeted = [sibling] + [at(dz=dz) for dz in (2, 6, 1, 7)] + [at(dy=dy) for dy in FOUR]
    greeted += [across(dx) for dx in FOUR]
    for device in greeted:
        pl.semaphore_signal(barrier, inc=1, device_id=device, device_id_type=MESH)

    def remote(src, dst, phase, device):
        return pltpu.make_async_remote_copy(
            src_ref=src,
            dst_ref=dst,
            send_sem=send_sems.at[phase],
            recv_sem=recv_sems.at[phase],
            device_id=device,
            device_id_type=MESH,
        )

    def arrived(ref, phase):
        remote(ref, ref, phase, sibling).wait_recv()

    def sent(ref, phase):
        remote(ref, ref, phase, sibling).wait_send()

    lane = lax.broadcasted_iota(jnp.int32, (8, 128), 1)
    excitation = lax.broadcasted_iota(jnp.int32, (8, 128), 0)

    def row_of(fields):
        total = jnp.zeros((8, 128), F32)
        for index, field in enumerate(fields):
            total = total + jnp.where(lane == index * 8 + excitation, field, 0.0)
        return jnp.sum(total, axis=0, keepdims=True)

    def column_of(row):
        return lane_sum(jnp.where(lane == excitation, row, 0.0))

    def project(value):
        high, low = halves(value)
        both = jnp.zeros((16, 512), F32)
        rest = jnp.zeros((8, 512), F32)
        stack = stacked([high, low])
        for region in range(2):
            columns = slice(1024 * region, 1024 * (region + 1))
            both = both + dot_nn(stack[:, columns], u_high[region])
            rest = rest + dot_nn(high[:, columns], u_low[region])
        return both[:8] + both[8:] + rest

    def expand(coeffs):
        high, low = halves(coeffs)
        stack = stacked([high, low])
        results = []
        for region in range(2):
            both = dot_nt(stack, u_high[region])
            results.append(both[:8] + both[8:] + dot_nt(high, u_low[region]))
        return jnp.concatenate(results, axis=1)

    def send_stats(index, phase, fields):
        row_ref[index] = row_of(fields)
        stat_ref[index, pl.ds(chip, 1), :] = row_ref[index]
        for dz, dy in PARTNERS[:-1]:
            remote(
                row_ref.at[index], stat_ref.at[index, pl.ds(chip, 1), :], phase, at(dz, dy)
            ).start()

    def read_stats(index, phase):
        arrived(stat_ref.at[index, pl.ds(0, 31), :], phase)
        return stat_ref[index]

    def all_reduce(m, partial, between, row=None, later=None):
        base = m * PHASES
        y_ref[m, 0] = partial
        for dy in FOUR:
            remote(y_ref.at[m, 0], y_ref.at[m, dy], base + YAX, at(dy=dy)).start()
        if row is not None:
            line_ref[0] = row()
            for dy in FOUR:
                remote(line_ref.at[0], line_ref.at[dy], base + ROW_Y, at(dy=dy)).start()
        between()
        arrived(y_ref.at[m, pl.ds(1, 3)], base + YAX)
        zax_ref[m, 0] = (y_ref[m, 0] + y_ref[m, 1]) + (y_ref[m, 2] + y_ref[m, 3])
        if m == 0:
            pl.semaphore_wait(ready_sem, 2)
        for dz in EIGHT:
            remote(zax_ref.at[m, 0], zax_ref.at[m, dz], base + ZAX, at(dz=dz)).start()
        if row is not None:
            arrived(line_ref.at[pl.ds(1, 3)], base + ROW_Y)
            line_ref[4] = (line_ref[0] + line_ref[1]) + (line_ref[2] + line_ref[3])
            for dz in EIGHT:
                remote(line_ref.at[4], line_ref.at[4 + dz], base + ROW_Z, at(dz=dz)).start()
            later()
            arrived(line_ref.at[pl.ds(5, 7)], base + ROW_Z)
            pairs = [line_ref[4 + 2 * i] + line_ref[5 + 2 * i] for i in range(4)]
            row = (pairs[0] + pairs[1]) + (pairs[2] + pairs[3])
        arrived(zax_ref.at[m, pl.ds(1, 7)], base + ZAX)
        pairs = [zax_ref[m, 2 * i] + zax_ref[m, 2 * i + 1] for i in range(4)]
        return (pairs[0] + pairs[1]) + (pairs[2] + pairs[3]), row

    def operate(m):
        base = m * PHASES
        field = z_ref[m]
        low = field.astype(BF16)
        charges = []
        for region in range(2):
            for half in range(2):
                start = 1024 * region + 512 * half
                part = low[:, start : start + 512]
                charges.append(
                    dot_nt(part, pick_ref[region, half]) + dot_nt(part, put_ref[region, half])
                )
        for quarter in range(4):
            first_region, second_region = charges[quarter // 2], charges[2 + quarter // 2]
            if quarter % 2:
                first_region = pltpu.roll(first_region, 64, 1)
            else:
                second_region = pltpu.roll(second_region, 64, 1)
            charge_out[m, quarter] = jnp.where(lane < 64, first_region, second_region)
        for dx in FOUR:
            remote(
                charge_out.at[m, groups[dx]], charge_in.at[m, x], base + CHARGE, across(dx)
            ).start()
        charge_in[m, x] = charge_out[m, x]

        for i in range(16):
            block = field[:, 128 * i : 128 * (i + 1)]
            blocks_ref[m, i] = block
            ext_ref[m, 8 * oc + i, c] = block
        remote(
            blocks_ref.at[m], ext_ref.at[m, pl.ds(8 * c, 16), c], base + NEAR, sibling
        ).start()
        remote(
            blocks_ref.at[m, pl.ds(0, 8)],
            ext_ref.at[m, pl.ds(16, 8), c],
            base + NEAR,
            (((chip + 31) % 32) * 2 + 1, x),
        ).start()
        remote(
            blocks_ref.at[m, pl.ds(8, 8)],
            ext_ref.at[m, pl.ds(0, 8), c],
            base + NEAR,
            (((chip + 1) % 32) * 2, x),
        ).start()

        if m == 0:
            local(couple_ref.at[c], couple_ref.at[c], L_COUPLE).wait()
            remote(couple_ref.at[c], couple_ref.at[c], COUPLE, sibling).start()

        if m == 0:
            for region in range(2):
                for half in range(2):
                    panels = slice(512 * half, 512 * (half + 1))
                    skeletons = slice(128 * half, 128 * (half + 1))
                    total = jnp.zeros((128, 512), F32)
                    for restriction in (pick_ref, put_ref):
                        for factor in (u_high, u_low):
                            total = total + dot_nn(
                                restriction[region, half], factor[region, panels, :]
                            )
                    high, low_part = halves(total)
                    skel_high[region, skeletons, :] = high
                    skel_low[region, skeletons, :] = low_part

        arrived(charge_in.at[m, pl.ds(0, 3)], base + CHARGE)
        block = jnp.concatenate([charge_in[m, i] for i in range(4)], axis=0).astype(BF16)

        def columns_of(offsets):
            first = ORDER.index(offsets[0])
            return gather_ref.at[m, y, :, pl.ds(128 * first, 128 * len(offsets))]

        columns_of((0,))[...] = block
        for dz in EIGHT:
            remote(columns_of((0,)), columns_of((dz,)), base + LINE + dz, at(dz=dz)).start()
        for group in GROUPS:
            for dz in group:
                if dz:
                    arrived(columns_of((dz,)), base + LINE + dz)
            for dy in FOUR:
                remote(
                    columns_of(group), columns_of(group), base + PLANE + dy, at(dy=dy)
                ).start()

        if m == 0:
            for index in (L_NEAR, L_IDS, L_COUNT):
                loads[index].wait()
        arrived(ext_ref.at[m, pl.ds(0, 16)], base + NEAR)
        for b in range(8):
            total = jnp.zeros((16, 128), F32)
            for pair in range(4):
                sides = []
                for k in (2 * pair, 2 * pair + 1):
                    source = jnp.clip(ids_ref[b, k] - (s - 1) * 8, 0, 23)
                    live = (k < count_ref[b]).astype(F32)
                    found = ext_ref[m, source].reshape(16, 128)
                    sides.append((found * live).astype(BF16))
                mats = jnp.concatenate([near_ref[b, 2 * pair], near_ref[b, 2 * pair + 1]], axis=1)
                total = total + dot_nt(jnp.concatenate(sides, axis=1), mats)
            near_out[m, 0, b] = total[:8]
            near_out[m, 1, b] = total[8:]
        remote(near_out.at[m, oc], near_in.at[m, c], base + NEAR_BACK, sibling).start()

        if m == 0:
            arrived(couple_ref.at[oc], COUPLE)

        def multiply(row):
            return [dot_nt(gather_ref[m, row], couple_ref[side, row]) for side in range(2)]

        parts = multiply(y)
        near_in[m, c] = near_out[m, c]
        arrived(near_in.at[m, oc], base + NEAR_BACK)
        for region in range(2):
            for b in range(8):
                start = 1024 * region + 128 * b
                columns = slice(start, start + 128)
                own_coef = self_ref[region, :, 128 * b : 128 * (b + 1)]
                w_ref[:, columns] = own_coef * field[:, columns] + near_in[m, region, b]
        for dy in FOUR[::-1]:
            arrived(gather_ref.at[m, rows_on[4 - dy]], base + PLANE + dy)
            parts = [a + b for a, b in zip(parts, multiply(rows_on[4 - dy]))]
        for i in range(4):
            for side in range(2):
                far_out[m, i, side] = parts[side][8 * i : 8 * (i + 1)]
        for dx in FOUR:
            remote(far_out.at[m, groups[dx]], far_in.at[m, x], base + FAR, across(dx)).start()
        far_in[m, x] = far_out[m, x]
        projected = project(w_ref[...]) if m == 0 else None
        arrived(far_in.at[m, pl.ds(0, 3)], base + FAR)
        fars = [
            (far_in[m, 0, side] + far_in[m, 1, side]) + (far_in[m, 2, side] + far_in[m, 3, side])
            for side in range(2)
        ]
        if m == 0:
            for side in range(2):
                high, rest = halves(fars[side])
                both = dot_nn(stacked([high, rest]), skel_high[side])
                projected = projected + (both[:8] + both[8:] + dot_nn(high, skel_low[side]))

        def finish():
            results = []
            for side in range(2):
                for half in range(2):
                    part = fars[side][:, 128 * half : 128 * (half + 1)]
                    high, _ = halves(part)
                    rest_high, rest_low = halves(part - high.astype(F32))
                    stack = stacked([high, rest_high, rest_low])
                    spread_out = dot_nn(stack, pick_ref[side, half]) + dot_nn(
                        stack, put_ref[side, half]
                    )
                    results.append(spread_out[:8] + spread_out[8:16] + spread_out[16:])
            return w_ref[...] + jnp.concatenate(results, axis=1)

        return finish, projected

    loads[L_RHS].wait()
    rhs_high, rhs_low = halves(rhs_ref[...])
    partial = jnp.zeros((16, 512), F32)
    for part in range(4):
        rows, columns = slice(256 * part, 256 * (part + 1)), slice(256 * part, 256 * (part + 1))
        factor_loads[part].wait()
        factor_high, factor_low = halves(u_ref[rows, :])
        u_high[c, rows, :] = factor_high
        u_low[c, rows, :] = factor_low
        high, low = rhs_high[:, columns], rhs_low[:, columns]
        both = dot_nn(jnp.concatenate([high, low], axis=0), factor_high)
        partial = partial + (both[:16] + both[16:] + dot_nn(high, factor_low))

    part_ref[0] = partial[:8]
    part_ref[1] = partial[8:]
    pl.semaphore_wait(barrier, len(greeted))

    remote(part_ref.at[oc], sib_ref, PART, sibling).start()
    other_half = rhs_ref.at[pl.ds(pl.multiple_of(8 * oc, 8), 8), :]
    remote(other_half, both_ref.at[c], RHS, sibling).start()
    for dz in (2, 6):
        pl.semaphore_signal(ready_sem, inc=1, device_id=at(dz=dz), device_id_type=MESH)
    both_ref[c] = rhs_ref[pl.ds(pl.multiple_of(8 * c, 8), 8), :]

    for load in loads[1:]:
        load.start()

    arrived(sib_ref, PART)

    def norm_row():
        arrived(both_ref.at[oc], RHS)
        both = jnp.concatenate([both_ref[0], both_ref[1]], axis=1)
        return row_of([lane_sum(both * both)])

    def load_columns():
        for place, dz in enumerate(ORDER):
            for row in range(4):
                source = pl.multiple_of((lines[(8 - dz) % 8] * 4 + row) * 128, 128)
                local(
                    couple_hbm.at[:, pl.ds(source, 128)],
                    couple_ref.at[c, row, :, pl.ds(128 * place, 128)],
                    L_COUPLE,
                ).start()

    def share_rest():
        for index in (L_DIAG, L_SELF, L_INTERP, L_SKEL):
            loads[index].wait()
        pick_ref[c] = jnp.zeros((2, 128, 512), BF16)
        put_ref[c] = jnp.zeros((2, 128, 512), BF16)
        square = lax.broadcasted_iota(jnp.int32, (32, 32), 0)
        square = (square == lax.broadcasted_iota(jnp.int32, (32, 32), 1)).astype(F32)
        turned = dot_nt(square.astype(BF16), skel_ref[...].astype(F32).astype(BF16))
        panel = lax.broadcasted_iota(jnp.int32, (32, 128), 1).astype(F32)
        for b in range(8):
            rows = slice(32 * (b % 4), 32 * (b % 4 + 1))
            columns = slice(128 * (b % 4), 128 * (b % 4 + 1))
            chosen = (panel == turned[:, b : b + 1]).astype(F32)
            pick_ref[c, b // 4, rows, columns] = chosen.astype(BF16)
            put_ref[c, b // 4, rows, columns] = interp_ref[b]
        load_columns()

    def share_coupling():
        for ref, phase in (
            (u_high, HIGH), (u_low, LOW), (diag_ref, DIAG), (self_ref, SELF), (pick_ref, PICK),
            (put_ref, PUT),
        ):
            remote(ref.at[c], ref.at[c], phase, sibling).start()

    raw, total = all_reduce(
        0, part_ref[c] + sib_ref[...], share_rest, norm_row, share_coupling
    )
    for ref, phase in (
        (u_high, HIGH), (u_low, LOW), (diag_ref, DIAG), (self_ref, SELF), (pick_ref, PICK),
        (put_ref, PUT),
    ):
        arrived(ref.at[oc], phase)
    beta_row = jnp.sqrt(total + EPS)
    beta = column_of(beta_row)
    first = jnp.concatenate([both_ref[0], both_ref[1]], axis=1) / beta
    first_coeffs = raw / beta
    diag = jnp.concatenate([diag_ref[0], diag_ref[1]], axis=1)
    z_ref[0] = diag * first - expand(first_coeffs)
    norm_one = lane_sum(first * first)
    safe_one = jnp.where(norm_one > 1e-12, norm_one, 1.0)

    def along(inner, norm, safe):
        return jnp.where(norm > 1e-12, inner / safe, 0.0)

    finish, projected = operate(0)
    residues = []

    def first_stats():
        residue = finish()
        residues.append(residue)
        own = along(lane_sum(residue * first), norm_one, safe_one)
        rest = residue - own * first
        send_stats(
            1, PHASES + STAT, [own, lane_sum(rest * first), norm_one, lane_sum(rest * rest)]
        )

    raw, _ = all_reduce(1, projected, first_stats)
    residue = residues[0]
    stats = read_stats(1, PHASES + STAT)

    def fields_of(stats, count):
        return [stats] + [pltpu.roll(stats, 128 - 8 * i, 1) for i in range(1, count)]

    def rows_sum(value):
        return jnp.sum(value, axis=0, keepdims=True)

    own, cross, norm, rest = fields_of(stats, 4)
    h11_row = rows_sum(cross + own * norm)
    shift = own - h11_row
    square = rows_sum(rest + 2.0 * shift * cross + shift * shift * norm)
    h21_row = jnp.sqrt(jnp.maximum(square, 0.0) + EPS)
    h11 = column_of(h11_row)
    h21 = column_of(h21_row)
    second = (residue - h11 * first) / h21
    second_coeffs = (raw - h11 * first_coeffs) / h21
    z_ref[1] = diag * second - expand(second_coeffs)
    norm_two = lane_sum(second * second)
    mixed = lane_sum(first * second)
    safe_two = jnp.where(norm_two > 1e-12, norm_two, 1.0)

    residue = operate(1)[0]()
    own_one = along(lane_sum(residue * first), norm_one, safe_one)
    rest = residue - own_one * first
    own_two = along(lane_sum(rest * second), norm_two, safe_two)
    rest = rest - own_two * second
    final_row[...] = row_of(
        [
            own_one, own_two, lane_sum(rest * first), lane_sum(rest * second),
            norm_one, mixed, norm_two, lane_sum(rest * rest), beta, h11, h21,
        ]
    )
    own_row = pl.ds(c * 32 + chip, 1)
    final_ref[own_row, :] = final_row[...]

    for dz, dy in PARTNERS:
        for core in (oc, c):
            if core is oc or dz or dy:
                target = (chips[dz][dy] * 2 + core, x)
                remote(final_row, final_ref.at[own_row, :], FINAL, target).start()

    sent(sib_ref, PART)
    sent(both_ref.at[c], RHS)
    for ref, phase in (
        (u_high, HIGH), (u_low, LOW), (diag_ref, DIAG), (self_ref, SELF), (pick_ref, PICK),
        (put_ref, PUT), (couple_ref, COUPLE),
    ):
        sent(ref.at[c], phase)
    sent(line_ref.at[pl.ds(1, 3)], ROW_Y)
    sent(line_ref.at[pl.ds(5, 7)], ROW_Z)
    sent(stat_ref.at[1, pl.ds(0, 31), :], PHASES + STAT)
    for m in range(2):
        base = m * PHASES
        sent(y_ref.at[m, pl.ds(1, 3)], base + YAX)
        sent(zax_ref.at[m, pl.ds(1, 7)], base + ZAX)
        sent(ext_ref.at[m, pl.ds(0, 16)], base + NEAR)
        sent(near_in.at[m, c], base + NEAR_BACK)
        sent(charge_in.at[m, pl.ds(0, 3)], base + CHARGE)
        for dz in EIGHT:
            sent(gather_ref.at[m, 0, :, pl.ds(0, 128)], base + LINE + dz)
        for dy in FOUR:
            sent(gather_ref.at[m, 0], base + PLANE + dy)
        sent(far_in.at[m, pl.ds(0, 3)], base + FAR)
    arrived(final_ref.at[pl.ds(0, 63), :], FINAL)
    sent(final_ref.at[pl.ds(0, 63), :], FINAL)

    for half in range(2):
        (
            own_one, own_two, cross_one, cross_two, n11, n12, n22, rest, beta_row, h11_row, h21_row
        ) = fields_of(final_ref[32 * half : 32 * (half + 1), :], 11)
        beta_row, h11_row, h21_row = beta_row[:1], h11_row[:1], h21_row[:1]
        h12_row = rows_sum(cross_one + own_one * n11 + own_two * n12)
        h22_row = rows_sum(cross_two + own_one * n12 + own_two * n22)
        shift_one = own_one - h12_row
        shift_two = own_two - h22_row
        square = rows_sum(
            rest
            + 2.0 * (shift_one * cross_one + shift_two * cross_two)
            + shift_one * shift_one * n11
            + 2.0 * shift_one * shift_two * n12
            + shift_two * shift_two * n22
        )
        h32_row = jnp.sqrt(jnp.maximum(square, 0.0) + EPS)
        radius_one = jnp.sqrt(h11_row * h11_row + h21_row * h21_row)
        cos_one = h11_row / radius_one
        sin_one = h21_row / radius_one
        upper = cos_one * h12_row + sin_one * h22_row
        lower = cos_one * h22_row - sin_one * h12_row
        radius_two = jnp.sqrt(lower * lower + h32_row * h32_row)
        step_two = lower / radius_two * (-sin_one * beta_row) / radius_two
        step_one = (cos_one * beta_row - upper * step_two) / radius_one
        column_one, column_two = column_of(step_one), column_of(step_two)
        for b in range(8):
            out_ref[8 * half : 8 * (half + 1), 128 * b : 128 * (b + 1)] = (
                column_one * ext_ref[0, 8 + b, half] + column_two * ext_ref[1, 8 + b, half]
            )


def hbm(value):
    return pltpu.with_memory_space_constraint(value, pltpu.HBM)


def on_device(
    rhs_vec, self_coef, near_mats, near_ids, near_count, interp, skel_idx, coupling,
    diag_prec, low_rank,
):
    vmem = pltpu.VMEM
    return pl.pallas_call(
        kernel,
        out_shape=jax.ShapeDtypeStruct((16, 1024), F32),
        in_specs=[pl.BlockSpec(memory_space=pltpu.HBM)] * 10,
        out_specs=pl.BlockSpec(memory_space=pltpu.VMEM),
        scratch_shapes=[
            vmem((16, 1024), F32),
            vmem((2, 1, 1024), F32),
            vmem((8, 8, 128, 128), BF16),
            pltpu.SMEM((8, 8), jnp.int32),
            pltpu.SMEM((8,), jnp.int32),
            vmem((8, 32, 128), BF16),
            vmem((8, 32), jnp.int32),
            vmem((2, 4, 256, 1024), BF16),
            vmem((2, 1, 1024), F32),
            vmem((1024, 512), F32),
            vmem((2, 1024, 512), BF16),
            vmem((2, 1024, 512), BF16),
            vmem((2, 256, 512), BF16),
            vmem((2, 256, 512), BF16),
            vmem((2, 2, 128, 512), BF16),
            vmem((2, 2, 128, 512), BF16),
            vmem((2, 8, 2048), F32),
            vmem((8, 2048), F32),
            vmem((2, 8, 512), F32),
            vmem((8, 512), F32),
            vmem((2, 8, 1024), F32),
            vmem((2, 4, 8, 512), F32),
            vmem((2, 8, 8, 512), F32),
            vmem((12, 1, 128), F32),
            vmem((3, 1, 128), F32),
            vmem((3, 32, 128), F32),
            vmem((2, 16, 8, 128), F32),
            vmem((2, 24, 2, 8, 128), F32),
            vmem((2, 2, 8, 8, 128), F32),
            vmem((2, 2, 8, 8, 128), F32),
            vmem((2, 4, 8, 128), F32),
            vmem((2, 4, 8, 128), F32),
            vmem((2, 4, 32, 1024), BF16),
            vmem((2, 4, 2, 8, 256), F32),
            vmem((2, 4, 2, 8, 256), F32),
            vmem((1, 128), F32),
            vmem((64, 128), F32),
            pltpu.SemaphoreType.DMA((FINAL + 1,)),
            pltpu.SemaphoreType.DMA((FINAL + 1,)),
            pltpu.SemaphoreType.DMA((L_U + 4,)),
            pltpu.SemaphoreType.REGULAR,
        ],
        compiler_params=pltpu.CompilerParams(
            collective_id=0, has_side_effects=True, vmem_limit_bytes=24 * 1024 * 1024
        ),
        name="gmres",
    )(
        hbm(rhs_vec),
        hbm(self_coef.reshape(1, -1)),
        hbm(near_mats),
        hbm(near_ids),
        hbm(near_count),
        hbm(jnp.swapaxes(interp, 1, 2)),
        hbm(skel_idx),
        hbm(coupling.reshape(coupling.shape[0], coupling.shape[2])),
        hbm(diag_prec.reshape(1, -1)),
        hbm(low_rank),
    )


def solution(mesh):
    placed = (
        P("rhs", "space"),
        P("space"),
        P("space", None, None, None),
        P("space", None),
        P("space"),
        P("space", None, None),
        P("space", None),
        P("space", "rhs", None),
        P("space"),
        P("space", None),
    )
    return jax.shard_map(
        on_device, mesh=mesh, in_specs=placed, out_specs=P("rhs", "space"), check_vma=False
    )
```
